128 devices in a mesh: dom: 128 (over z, y, x, core).
Axes of the slice: x: 4, y: 4, z: 4, core: 2. Of those that a mesh axis runs over, the one named last changes fastest.
Arguments:
- a_blocks: bfloat16 [3072, 64, 448], P('dom'), may hold values from -0.25 to 0.25
- p_blocks: bfloat16 [3072, 64, 1728], P('dom'), may hold values from -0.59765625 to 0.59765625
- cols_a: int32 [3072, 7], P('dom'), may hold values from 0 to 3071, as said below
- cols_p: int32 [3072, 27], P('dom'), may hold values from 0 to 383, as said below
Outputs:
- coarse_op: float32 [384, 64, 4032], P('dom')
The draws below stay inside these ranges and needn't reach their ends.
Inputs may be any that keep to these rules, and one draw needn't show every extreme that they name: `cols_a`: row e lists e itself first, then 7 - 1 other distinct rows, all in the aggregates agg(e) - 1, agg(e) and agg(e) + 1, counted cyclically. `cols_p`: the 27 entries of a row are distinct aggregates within 15 of the row's own aggregate, counted cyclically.
All inputs are finite; a program needn't handle non-finite values.
Results may differ from the reference program's by a relative error of at most 0.0041.
Values may be sent and summed in bfloat16 or wider, within the bound.
A program may use at most 192 MiB of HBM per device.

```python
import jax
import jax.numpy as jnp
from jax import lax

BS = 64
KA = 7
KP = 27
AGG = 8
H = 15
NC = 3
NB = 24
NF = 3072
NCT = 384
WIN = 31
WSLOT = 33
BAND = 63
N_DOM = 128


def pick_rows(row_key):
    return jax.random.permutation(row_key, 3 * AGG - 1)[:KA - 1]


def pick_aggs(row_key):
    return jax.random.permutation(row_key, WIN)[:KP]


def draw_cols_a(key, part):
    row_ids = jnp.arange(NF, dtype=jnp.int32)
    row_keys = jax.random.split(jax.random.fold_in(key, 11), NF)
    picks = jax.vmap(pick_rows)(row_keys).astype(jnp.int32)
    own_pos = AGG + row_ids % AGG
    picks = picks + (picks >= own_pos[:, None]).astype(jnp.int32)
    base_row = (row_ids // AGG - 1) * AGG
    others = (base_row[:, None] + picks) % NF
    return jnp.concatenate([row_ids[:, None], others], axis=1).astype(jnp.int32)


def draw_cols_p(key, part):
    row_ids = jnp.arange(NF, dtype=jnp.int32)
    row_keys = jax.random.split(jax.random.fold_in(key, 23), NF)
    picks = jax.vmap(pick_aggs)(row_keys).astype(jnp.int32)
    own_agg = row_ids // AGG
    return ((own_agg[:, None] - H + picks) % NCT).astype(jnp.int32)


def block_scale(rng, extent, shards, least, top_value):
    loudness = 1.0
    for dim, shards_of in shards:
        steps = jax.random.uniform(jax.random.fold_in(jax.random.fold_in(rng, 6), dim), (shards_of,), jnp.float32, least / len(shards), top_value / len(shards))
        loudness = loudness * jnp.repeat(jnp.exp(steps), extent[dim] // shards_of).reshape((-1,) + (1,) * (len(extent) - 1 - dim))
    return loudness


def gaussian(own_key, extent, deviation, reach, shards=(), kind=jnp.bfloat16):
    array = deviation * jax.random.normal(own_key, extent, jnp.float32)
    if shards:
        array = array * block_scale(own_key, extent, shards, -0.22, 0.18)
    return jnp.clip(array, -reach, reach).astype(kind)


def setup_inputs(seed: int = 0) -> dict:
    seeds = jax.random.split(jax.random.key(seed), 5)
    return {
        "a_blocks": gaussian(seeds[0], (NF, BS, KA * BS), (KA * BS) ** -0.5, 0.25, ((0, 128),)),
        "p_blocks": gaussian(seeds[1], (NF, BS, KP * BS), 0.1, 0.59765625, ((0, 128),)),
        "cols_a": draw_cols_a(jax.random.fold_in(seeds[4], 71), 0),
        "cols_p": draw_cols_p(jax.random.fold_in(seeds[4], 71), 0),
    }


def band_form(p_rows, cols_rows, first_agg, count_agg):
    row_count = p_rows.shape[0]
    own_agg = (first_agg + jnp.arange(row_count, dtype=jnp.int32) // AGG) % count_agg
    offset = (cols_rows - own_agg[:, None] + H) % count_agg
    picker = (offset[:, :, None] == jnp.arange(WIN, dtype=jnp.int32)[None, None, :]).astype(jnp.float32)
    shaped = p_rows.reshape(row_count, BS, KP, BS).astype(jnp.float32)
    banded = jnp.einsum("riqc,rqs->risc", shaped, picker)
    return banded.astype(jnp.bfloat16).reshape(row_count, BS, WIN * BS)


def reference(a_blocks, p_blocks, cols_a, cols_p):
    count_agg = NC * N_DOM
    count_rows = NB * N_DOM

    def device_step(coarse, device):
        first_agg = device * NC
        first_row = device * NB
        ext_index = (first_row - AGG + jnp.arange(NB + 2 * AGG, dtype=jnp.int32)) % count_rows
        ext_band = band_form(p_blocks[ext_index], cols_p[ext_index], first_agg - 1, count_agg)
        own_band = ext_band[AGG:AGG + NB]
        padded = jnp.pad(ext_band, ((0, 0), (0, 0), (2 * BS, 2 * BS)))
        own_cols = lax.dynamic_slice_in_dim(cols_a, first_row, NB, 0)
        row_ids = first_row + jnp.arange(NB, dtype=jnp.int32)
        local_cols = (own_cols - first_row + AGG) % count_rows
        agg_shift = (own_cols // AGG - (row_ids // AGG)[:, None] + 1) % count_agg
        start_slot = (2 - agg_shift) * BS

        def frame_one(row_index, slot_index):
            zero_index = jnp.zeros((), jnp.int32)
            return lax.dynamic_slice(padded, (row_index.astype(jnp.int32), zero_index, slot_index.astype(jnp.int32)), (1, BS, WSLOT * BS))[0]

        frames = jax.vmap(jax.vmap(frame_one))(local_cols, start_slot)
        own_a = lax.dynamic_slice_in_dim(a_blocks, first_row, NB, 0).reshape(NB, BS, KA, BS)
        widened = jnp.einsum("eikj,ekjw->eiw", own_a.astype(jnp.float32), frames.astype(jnp.float32)).astype(jnp.bfloat16)
        p_group = own_band.reshape(NC, AGG * BS, WIN * BS).astype(jnp.float32)
        w_group = widened.reshape(NC, AGG * BS, WSLOT * BS).astype(jnp.float32)
        products = jnp.einsum("akx,aky->axy", p_group, w_group)
        partial_value = jnp.zeros(((NC + 2 * H) * BS, (NC + 2 * H + 2) * BS), jnp.float32)
        for local_agg in range(NC):
            offset = local_agg * BS
            partial_value = partial_value.at[offset:offset + WIN * BS, offset:offset + WSLOT * BS].add(products[local_agg])
        rounded = lax.optimization_barrier(partial_value.astype(jnp.bfloat16)).astype(jnp.float32)
        rows_band = rounded.reshape(NC + 2 * H, BS, (NC + 2 * H + 2) * BS)
        wide_cols = jnp.pad(rows_band, ((0, 0), (0, 0), (2 * H * BS, BAND * BS)))

        def skew_row(row_block, position):
            return lax.dynamic_slice_in_dim(row_block, position * BS, BAND * BS, 1)

        skewed = jax.vmap(skew_row)(wide_cols, jnp.arange(NC + 2 * H, dtype=jnp.int32))
        coarse_rows = (first_agg - H + jnp.arange(NC + 2 * H, dtype=jnp.int32)) % count_agg
        return coarse.at[coarse_rows].add(skewed), None

    start = jnp.zeros((count_agg, BS, BAND * BS), jnp.float32)
    coarse, unused = lax.scan(device_step, start, jnp.arange(N_DOM, dtype=jnp.int32))
    return coarse
```

```python
import functools

import jax
import jax.numpy as jnp
from jax import lax
from jax.experimental import pallas as pl
from jax.experimental.pallas import tpu as pltpu
from jax.sharding import PartitionSpec as P

BS = 64
KA = 7
KP = 27
AGG = 8
H = 15
NC = 3
NB = 24
WIN = 31
BAND = 63
REACH = 5
MESH = pl.DeviceIdType.MESH

ROWS = AGG * BS
FRAME = 36 * BS
SLAB = 32 * BS
WIDE = 48 * BS
TOTAL = 66 * BS
WIDTHS = [36 * BS, 40 * BS, 42 * BS, 46 * BS, 48 * BS]
GROUP = NC * BS
CHUNK = 256
F32 = jnp.float32
BF16 = jnp.bfloat16


def tables(cols_a, cols_p, device, count_agg):
    odd = device % 2
    agg_here = jnp.arange(NB, dtype=jnp.int32) // AGG
    slot = (cols_p - (device * NC + agg_here)[:, None] + H) % count_agg
    frame = slot + agg_here[:, None] + 1 + odd
    slab = slot + (1 - odd)
    target = jnp.concatenate([frame, slab[:AGG], slab[NB - AGG :]], axis=0)

    def tile_of(target, count, blocks, tiles):
        spots = jnp.arange(count, dtype=jnp.int32)
        order = jnp.arange(blocks, dtype=jnp.int32)
        hit = target[:, :, None] == spots[None, None, :]
        found = blocks + jnp.sum(jnp.where(hit, order[None, :, None] - blocks, 0), axis=1)
        return ((found ^ spots[None, :]) & 1) * tiles + (found >> 1)

    fine = (cols_a - ((device * NC + agg_here - 1) * AGG)[:, None]) % (count_agg * AGG)
    p_tile = tile_of(target, 36, KP, 14)
    a_tile = tile_of(fine, 24, KA, 4)
    return jnp.concatenate([p_tile, jnp.pad(a_tile, ((0, 0), (0, 12)))], axis=0)


def swap_halves(x):
    return jnp.concatenate([x[:, BS:], x[:, :BS]], axis=1)


def band_kernel(tab, p_ref, a_ref, own_ref, slab_ref, turned_ref, dense_ref, p2, a2):
    agg = pl.program_id(0)
    low = lax.broadcasted_iota(jnp.int32, (BS, 128), 1) < BS

    def double(src, dst, wide, tiles):
        def step(e, _):
            dst[e, :, :wide] = src[e]
            dst[e, :, wide : 128 * tiles] = jnp.zeros((BS, 128 * tiles - wide), BF16)
            for tile in range(tiles):
                here = dst[e, :, 128 * tile : 128 * tile + 128]
                dst[e, :, 128 * (tiles + tile) : 128 * (tiles + tile + 1)] = swap_halves(here)
            return 0

        lax.fori_loop(0, AGG, step, 0)

    double(p_ref, p2, KP * BS, 14)
    double(a_ref, a2, KA * BS, 4)

    def place(src, dst, first, pairs):
        def step(e, _):
            for pair in range(pairs):
                left = pl.multiple_of(tab[first + e, 2 * pair] * 128, 128)
                right = pl.multiple_of(tab[first + e, 2 * pair + 1] * 128, 128)
                both = jnp.where(low, src[e, :, pl.ds(left, 128)], src[e, :, pl.ds(right, 128)])
                dst[e, :, 128 * pair : 128 * pair + 128] = both
            return 0

        lax.fori_loop(0, AGG, step, 0)

    @pl.when(agg != 1)
    def _():
        place(p2, slab_ref, NB + 4 * agg, 16)

    place(p2, own_ref, AGG * agg, 18)
    place(a2, dense_ref, NB + 2 * AGG + AGG * agg, 12)
    for tile in range(18):
        here = own_ref[:, :, 128 * tile : 128 * tile + 128].reshape(ROWS, 128)
        turned_ref[128 * tile : 128 * tile + 128, :] = here.T


def band(tab, p_blocks, a_blocks):
    return pl.pallas_call(
        band_kernel,
        out_shape=(
            jax.ShapeDtypeStruct((NB, BS, FRAME), BF16),
            jax.ShapeDtypeStruct((2 * AGG, BS, SLAB), BF16),
            jax.ShapeDtypeStruct((FRAME, NB * BS), BF16),
            jax.ShapeDtypeStruct((NB, BS, 3 * ROWS), BF16),
        ),
        grid_spec=pltpu.PrefetchScalarGridSpec(
            num_scalar_prefetch=1,
            grid=(NC,),
            in_specs=[
                pl.BlockSpec((AGG, BS, KP * BS), lambda i, t: (i, 0, 0)),
                pl.BlockSpec((AGG, BS, KA * BS), lambda i, t: (i, 0, 0)),
            ],
            out_specs=[
                pl.BlockSpec((AGG, BS, FRAME), lambda i, t: (i, 0, 0)),
                pl.BlockSpec((AGG, BS, SLAB), lambda i, t: (i // 2, 0, 0)),
                pl.BlockSpec((FRAME, ROWS), lambda i, t: (0, i)),
                pl.BlockSpec((AGG, BS, 3 * ROWS), lambda i, t: (i, 0, 0)),
            ],
            scratch_shapes=[
                pltpu.VMEM((AGG, BS, 2 * 14 * 128), BF16),
                pltpu.VMEM((AGG, BS, 2 * 4 * 128), BF16),
            ],
        ),
        compiler_params=pltpu.CompilerParams(vmem_limit_bytes=48 * 2**20),
    )(tab, p_blocks, a_blocks)


def dot(a, b):
    return jnp.dot(a, b, preferred_element_type=F32)


def chain_kernel(
    count, own, slab, turned, dense, out,
    ext, pt, ad, w, wf, part, rb, lb, tot,
    load_sem, halo_send, halo_recv, send_r, recv_r, send_l, recv_l,
):
    me = lax.axis_index("dom")
    right, left = lax.rem(me + 1, count), lax.rem(me + count - 1, count)
    odd = lax.rem(me, 2)

    barrier = pltpu.get_barrier_semaphore()
    for neighbour in (left, right):
        pl.semaphore_signal(barrier, inc=1, device_id=(neighbour,), device_id_type=MESH)
    pl.semaphore_wait(barrier, 2)

    halos = [
        pltpu.make_async_remote_copy(
            src_ref=slab.at[pl.ds(ROWS, ROWS)],
            dst_ref=ext.at[pl.ds(0, ROWS), pl.ds(0, SLAB)],
            send_sem=halo_send.at[0],
            recv_sem=halo_recv.at[0],
            device_id=(right,),
            device_id_type=MESH,
        ),
        pltpu.make_async_remote_copy(
            src_ref=slab.at[pl.ds(0, ROWS)],
            dst_ref=ext.at[pl.ds(4 * ROWS, ROWS), pl.ds(4 * BS, SLAB)],
            send_sem=halo_send.at[1],
            recv_sem=halo_recv.at[1],
            device_id=(left,),
            device_id_type=MESH,
        ),
    ]
    for copy in halos:
        copy.start()
    loads = [
        pltpu.make_async_copy(own, ext.at[pl.ds(ROWS, 3 * ROWS)], load_sem.at[0]),
        pltpu.make_async_copy(dense, ad, load_sem.at[1]),
        pltpu.make_async_copy(turned, pt, load_sem.at[2]),
    ]
    for copy in loads:
        copy.start()

    ext[:ROWS, SLAB:] = jnp.zeros((ROWS, FRAME - SLAB), BF16)
    ext[4 * ROWS :, : 4 * BS] = jnp.zeros((ROWS, 4 * BS), BF16)
    for step in range(1, REACH):
        before, after = WIDTHS[step - 1], WIDTHS[step]
        rb[step, :, before:after] = jnp.zeros((GROUP, after - before), BF16)
        lb[step, :, WIDE - after : WIDE - before] = jnp.zeros((GROUP, after - before), BF16)

    def chunks(body):
        def step(n, _):
            body(pl.multiple_of(n * CHUNK, CHUNK))
            return 0

        lax.fori_loop(0, FRAME // CHUNK, step, 0)

    loads[0].wait()
    loads[1].wait()

    def inner(at):
        cols = pl.ds(at, CHUNK)
        w[ROWS : 2 * ROWS, cols] = dot(ad[ROWS : 2 * ROWS, :], ext[ROWS : 4 * ROWS, cols]).astype(BF16)
        wf[:ROWS, cols] = dot(ad[:ROWS, ROWS:], ext[ROWS : 3 * ROWS, cols])
        wf[ROWS:, cols] = dot(ad[2 * ROWS :, : 2 * ROWS], ext[2 * ROWS : 4 * ROWS, cols])

    chunks(inner)
    loads[2].wait()
    halos[0].wait_recv()

    def first(at):
        cols = pl.ds(at, CHUNK)
        more = dot(ad[:ROWS, :ROWS], ext[:ROWS, cols])
        w[:ROWS, cols] = (wf[:ROWS, cols] + more).astype(BF16)

    chunks(first)
    halos[1].wait_recv()

    def last(at):
        cols = pl.ds(at, CHUNK)
        more = dot(ad[2 * ROWS :, 2 * ROWS :], ext[4 * ROWS :, cols])
        w[2 * ROWS :, cols] = (wf[ROWS:, cols] + more).astype(BF16)

    chunks(last)

    def product(group, at):
        rows = pl.ds(pl.multiple_of((NC * group + 1 + odd) * BS, BS), GROUP)
        return dot(pt[rows, :], w[:, pl.ds(at, CHUNK)]).astype(BF16)

    def send(step):
        width = WIDTHS[step]
        pair = []
        for buf, begin, sends, recvs, target in (
            (rb, 0, send_r, recv_r, right),
            (lb, WIDE - width, send_l, recv_l, left),
        ):
            copy = pltpu.make_async_remote_copy(
                src_ref=buf.at[step, :, pl.ds(begin, width)],
                dst_ref=buf.at[step + 1, :, pl.ds(begin, width)],
                send_sem=sends.at[step],
                recv_sem=recvs.at[step],
                device_id=(target,),
                device_id_type=MESH,
            )
            copy.start()
            pair.append(copy)
        return pair

    def ends(at):
        cols = pl.ds(at, CHUNK)
        rb[0, :, cols] = product(2 * REACH, at)
        lb[0, :, pl.ds(pl.multiple_of(at + WIDE - FRAME, 128), CHUNK)] = product(0, at)

    chunks(ends)
    sent = [send(0)]
    for step in range(1, REACH):
        reach = REACH - step

        def both(at):
            cols = pl.ds(at, CHUNK)
            part[0, :, cols] = product(REACH + reach, at)
            part[1, :, cols] = product(REACH - reach, at)

        chunks(both)
        if step % 2:
            shift_r = 3 * step + 1 - 2 * odd
            shift_l = 12 - (3 * step - 1 + 2 * odd)
        else:
            shift_r, shift_l = 3 * step, 12 - 3 * step
        for side, (buf, shift) in enumerate(((rb, shift_r), (lb, shift_l))):
            sent[step - 1][side].wait_recv()

            def add(at):
                cols = pl.ds(pl.multiple_of(at + shift * BS, 128), CHUNK)
                summed = buf[step, :, cols].astype(F32) + part[side, :, pl.ds(at, CHUNK)].astype(F32)
                buf[step, :, cols] = summed.astype(BF16)

            chunks(add)
        sent.append(send(step))

    def middle(at):
        part[0, :, pl.ds(at, CHUNK)] = product(REACH, at)

    chunks(middle)
    tot[:, : 18 * BS] = jnp.zeros((GROUP, 18 * BS), F32)
    tot[:, 52 * BS :] = jnp.zeros((GROUP, 14 * BS), F32)
    tot[:, 18 * BS : 52 * BS] = jnp.zeros((GROUP, 34 * BS), F32)

    def put(at):
        cols = pl.ds(pl.multiple_of(at + (16 - 2 * odd) * BS, 128), CHUNK)
        tot[:, cols] = part[0, :, pl.ds(at, CHUNK)].astype(F32)

    chunks(put)
    sent[REACH - 1][0].wait_recv()
    tot[:, :WIDE] += rb[REACH].astype(F32)
    sent[REACH - 1][1].wait_recv()
    tot[:, 18 * BS :] += lb[REACH].astype(F32)
    for parity in (0, 1):

        @pl.when(odd == parity)
        def _():
            for row in range(NC):
                start = (row + 1 - parity) * BS
                out[row] = tot[row * BS : (row + 1) * BS, start : start + BAND * BS]

    for copy in halos:
        copy.wait_send()
    for pair in sent:
        for copy in pair:
            copy.wait_send()


def chain(count, own, slab, turned, dense):
    anywhere = pl.BlockSpec(memory_space=pl.ANY)
    return pl.pallas_call(
        functools.partial(chain_kernel, count),
        out_shape=jax.ShapeDtypeStruct((NC, BS, BAND * BS), F32),
        in_specs=[anywhere] * 4,
        out_specs=pl.BlockSpec(memory_space=pltpu.VMEM),
        scratch_shapes=[
            pltpu.VMEM((5 * ROWS, FRAME), BF16),
            pltpu.VMEM((FRAME, 3 * ROWS), BF16),
            pltpu.VMEM((3 * ROWS, 3 * ROWS), BF16),
            pltpu.VMEM((3 * ROWS, FRAME), BF16),
            pltpu.VMEM((2 * ROWS, FRAME), F32),
            pltpu.VMEM((2, GROUP, FRAME), BF16),
            pltpu.VMEM((REACH + 1, GROUP, WIDE), BF16),
            pltpu.VMEM((REACH + 1, GROUP, WIDE), BF16),
            pltpu.VMEM((GROUP, TOTAL), F32),
            pltpu.SemaphoreType.DMA((3,)),
            pltpu.SemaphoreType.DMA((2,)),
            pltpu.SemaphoreType.DMA((2,)),
            pltpu.SemaphoreType.DMA((REACH,)),
            pltpu.SemaphoreType.DMA((REACH,)),
            pltpu.SemaphoreType.DMA((REACH,)),
            pltpu.SemaphoreType.DMA((REACH,)),
        ],
        compiler_params=pltpu.CompilerParams(
            collective_id=0, has_side_effects=True, vmem_limit_bytes=63 * 2**20
        ),
    )(own, slab, turned, dense)


def body(a_blocks, p_blocks, cols_a, cols_p):
    count = lax.axis_size("dom")
    tab = tables(cols_a, cols_p, lax.axis_index("dom"), NC * count)
    own, slab, turned, dense = band(tab, p_blocks, a_blocks)
    return chain(
        count,
        own.reshape(3 * ROWS, FRAME),
        slab.reshape(2 * ROWS, SLAB),
        turned,
        dense.reshape(3 * ROWS, 3 * ROWS),
    )


def solution(mesh):
    in_specs = (P("dom", None, None), P("dom", None, None), P("dom", None), P("dom", None))
    out_specs = P("dom", None, None)
    return jax.shard_map(body, mesh=mesh, in_specs=in_specs, out_specs=out_specs, check_vma=False)
```

```python
import functools

import jax
import jax.numpy as jnp
from jax import lax
from jax.experimental import pallas as pl
from jax.experimental.pallas import tpu as pltpu
from jax.sharding import PartitionSpec as P

BS = 64
KA = 7
KP = 27
AGG = 8
H = 15
NC = 3
NB = 24
WIN = 31
BAND = 63
REACH = 5
MESH = pl.DeviceIdType.MESH

ROWS = AGG * BS
FRAME = 36 * BS
SLAB = 32 * BS
WIDE = 48 * BS
TOTAL = 66 * BS
WIDTHS = [36 * BS, 40 * BS, 42 * BS, 46 * BS, 48 * BS]
GROUP = NC * BS
CHUNK = 768
F32 = jnp.float32
BF16 = jnp.bfloat16


def tables(cols_a, cols_p, device, count_agg):
    odd = device % 2
    agg_here = jnp.arange(NB, dtype=jnp.int32) // AGG
    slot = (cols_p - (device * NC + agg_here)[:, None] + H) % count_agg
    frame = slot + agg_here[:, None] + 1 + odd
    slab = slot + (1 - odd)
    target = jnp.concatenate([frame, slab[:AGG], slab[NB - AGG :]], axis=0)

    def tile_of(target, count, blocks, tiles):
        spots = jnp.arange(count, dtype=jnp.int32)
        order = jnp.arange(blocks, dtype=jnp.int32)
        hit = target[:, :, None] == spots[None, None, :]
        found = blocks + jnp.sum(jnp.where(hit, order[None, :, None] - blocks, 0), axis=1)
        return ((found ^ spots[None, :]) & 1) * tiles + (found >> 1)

    fine = (cols_a - ((device * NC + agg_here - 1) * AGG)[:, None]) % (count_agg * AGG)
    p_tile = tile_of(target, 36, KP, 14)
    a_tile = tile_of(fine, 24, KA, 4)
    return jnp.concatenate([p_tile, jnp.pad(a_tile, ((0, 0), (0, 12)))], axis=0)


def swap_halves(x):
    return jnp.concatenate([x[:, BS:], x[:, :BS]], axis=1)


def dot(a, b):
    return jnp.dot(a, b, preferred_element_type=F32)


def aligned(value, multiple=128):
    return pl.multiple_of(value, multiple)


def doubled(src, first, dst, wide, tiles):
    def step(e, _):
        rows = pl.ds(aligned(e * BS, BS), BS)
        for tile in range(tiles):
            if 128 * (tile + 1) <= wide:
                here = src[first + e, :, 128 * tile : 128 * tile + 128]
            else:
                here = jnp.concatenate([src[first + e, :, 128 * tile : wide], jnp.zeros((BS, BS), BF16)], axis=1)
            dst[tile, rows, :] = here
            dst[tiles + tile, rows, :] = swap_halves(here)
        return 0

    lax.fori_loop(0, AGG, step, 0)


def place(tab, first, src, dst, dst_row, pairs):
    low = lax.broadcasted_iota(jnp.int32, (BS, 128), 1) < BS

    def step(e, _):
        rows = pl.ds(aligned(e * BS, BS), BS)
        to = pl.ds(aligned(dst_row + e * BS, BS), BS)
        for pair in range(pairs):
            left = src[tab[first + e, 2 * pair], rows, :]
            right = src[tab[first + e, 2 * pair + 1], rows, :]
            dst[to, 128 * pair : 128 * pair + 128] = jnp.where(low, left, right)
        return 0

    lax.fori_loop(0, AGG, step, 0)


def chain_kernel(count, tab, p_blocks, a_blocks, from_left, from_right, middle, *scratch):
    raw, raw_a, p2, a2, slab, ext, pt, ad, w, wf, part = scratch[:11]
    rb = [*scratch[11 : 11 + REACH], from_left]
    lb = [*scratch[11 + REACH : 11 + 2 * REACH], from_right]
    load_sem, halo_send, halo_recv, send_r, recv_r, send_l, recv_l = scratch[11 + 2 * REACH :]
    me = lax.axis_index("dom")
    odd = lax.rem(me, 2)
    right, left = lax.rem(me + 1, count), lax.rem(me + count - 1, count)
    far, near = lax.rem(me + count - 1 + 2 * odd, count), lax.rem(me + count + 1 - 2 * odd, count)
    far_agg, near_agg = 2 * odd, 2 - 2 * odd

    def load(agg, slot, sem):
        return pltpu.make_async_copy(p_blocks.at[pl.ds(AGG * agg, AGG)], raw.at[slot], load_sem.at[sem])

    loads = [load(far_agg, 0, 0), load(near_agg, 1, 1)]
    load_a = pltpu.make_async_copy(a_blocks, raw_a, load_sem.at[2])
    for copy in (*loads, load_a):
        copy.start()
    barrier = pltpu.get_barrier_semaphore()
    for neighbour in (left, right):
        pl.semaphore_signal(barrier, inc=1, device_id=(neighbour,), device_id_type=MESH)

    def halo(side, target, edge):
        return pltpu.make_async_remote_copy(
            src_ref=slab.at[side],
            dst_ref=ext.at[pl.ds(aligned(edge * 4 * ROWS), ROWS), pl.ds(aligned(edge * 4 * BS), SLAB)],
            send_sem=halo_send.at[side],
            recv_sem=halo_recv.at[side],
            device_id=(target,),
            device_id_type=MESH,
        )

    halos = [halo(0, far, 1 - odd), halo(1, near, odd)]

    def own(agg):
        place(tab, AGG * agg, p2, ext, ROWS + ROWS * agg, 18)

    loads[0].wait()
    doubled(raw.at[0], 0, p2, KP * BS, 14)
    place(tab, NB + 4 * far_agg, p2, slab.at[0], 0, 16)
    pl.semaphore_wait(barrier, 2)
    halos[0].start()
    inner_load = load(1, 0, 3)
    inner_load.start()
    own(far_agg)
    loads[1].wait()
    doubled(raw.at[1], 0, p2, KP * BS, 14)
    place(tab, NB + 4 * near_agg, p2, slab.at[1], 0, 16)
    halos[1].start()
    own(near_agg)
    inner_load.wait()
    doubled(raw.at[0], 0, p2, KP * BS, 14)
    own(1)
    load_a.wait()
    for agg in range(NC):
        doubled(raw_a, AGG * agg, a2, KA * BS, 4)
        place(tab, NB + 2 * AGG + AGG * agg, a2, ad, ROWS * agg, 12)

    ext[:ROWS, SLAB:] = jnp.zeros((ROWS, FRAME - SLAB), BF16)
    ext[4 * ROWS :, : 4 * BS] = jnp.zeros((ROWS, 4 * BS), BF16)
    for step in range(1, REACH):
        before, after = WIDTHS[step - 1], WIDTHS[step]
        rb[step][:, before:after] = jnp.zeros((GROUP, after - before), BF16)
        lb[step][:, : after - before] = jnp.zeros((GROUP, after - before), BF16)

    for agg in range(NC):

        def turn(tile, _):
            lanes = pl.ds(aligned(tile * 128), 128)
            pt[lanes, ROWS * agg : ROWS * (agg + 1)] = ext[ROWS * (agg + 1) : ROWS * (agg + 2), lanes].T
            return 0

        lax.fori_loop(0, FRAME // 128, turn, 0)

    def chunks(body):
        def step(n, _):
            body(aligned(n * CHUNK))
            return 0

        lax.fori_loop(0, FRAME // CHUNK, step, 0)

    far_rows = pl.ds(aligned(far_agg * ROWS), ROWS)
    near_rows = pl.ds(aligned(near_agg * ROWS), ROWS)

    def inner(at):
        cols = pl.ds(at, CHUNK)
        w[ROWS : 2 * ROWS, cols] = dot(ad[ROWS : 2 * ROWS, :], ext[ROWS : 4 * ROWS, cols]).astype(BF16)
        wf[:, cols] = dot(
            ad[far_rows, pl.ds(aligned(ROWS * (1 - odd)), 2 * ROWS)],
            ext[pl.ds(aligned(ROWS + ROWS * odd), 2 * ROWS), cols],
        )

    def near_side(at):
        cols = pl.ds(at, CHUNK)
        whole = dot(ad[near_rows, :], ext[pl.ds(aligned(2 * ROWS * (1 - odd)), 3 * ROWS), cols])
        w[near_rows, cols] = whole.astype(BF16)

    def far_side(at):
        cols = pl.ds(at, CHUNK)
        more = dot(
            ad[far_rows, pl.ds(aligned(2 * ROWS * odd), ROWS)],
            ext[pl.ds(aligned(4 * ROWS * odd), ROWS), cols],
        )
        w[far_rows, cols] = (wf[:, cols] + more).astype(BF16)

    chunks(inner)
    halos[1].wait_recv()
    chunks(near_side)
    halos[0].wait_recv()
    chunks(far_side)

    def product(group, at):
        rows = pl.ds(aligned((NC * group + 1 + odd) * BS, BS), GROUP)
        return dot(pt[rows, :], w[:, pl.ds(at, CHUNK)]).astype(BF16)

    def send(step):
        width = WIDTHS[step]
        begin = WIDTHS[min(step + 1, REACH - 1)] - width
        pair = []
        for buf, place_to, sends, recvs, target in (
            (rb, 0, send_r, recv_r, right),
            (lb, begin, send_l, recv_l, left),
        ):
            copy = pltpu.make_async_remote_copy(
                src_ref=buf[step],
                dst_ref=buf[step + 1].at[:, pl.ds(place_to, width)],
                send_sem=sends.at[step],
                recv_sem=recvs.at[step],
                device_id=(target,),
                device_id_type=MESH,
            )
            copy.start()
            pair.append(copy)
        return pair

    def ends(at):
        cols = pl.ds(at, CHUNK)
        rb[0][:, cols] = product(2 * REACH, at)
        lb[0][:, cols] = product(0, at)

    chunks(ends)
    sent = [send(0)]
    for step in range(1, REACH):
        reach = REACH - step

        def both(at):
            cols = pl.ds(at, CHUNK)
            part[0, :, cols] = product(REACH + reach, at)
            part[1, :, cols] = product(REACH - reach, at)

        chunks(both)
        spare = WIDTHS[step] // BS - 36
        if step % 2:
            shift_r = 3 * step + 1 - 2 * odd
            shift_l = spare - (3 * step - 1 + 2 * odd)
        else:
            shift_r, shift_l = 3 * step, spare - 3 * step
        for side, (buf, shift) in enumerate(((rb[step], shift_r), (lb[step], shift_l))):
            sent[step - 1][side].wait_recv()

            def add(at):
                cols = pl.ds(aligned(at + shift * BS), CHUNK)
                summed = buf[:, cols].astype(F32) + part[side, :, pl.ds(at, CHUNK)].astype(F32)
                buf[:, cols] = summed.astype(BF16)

            chunks(add)
        sent.append(send(step))

    def centre(at):
        part[0, :, pl.ds(at, CHUNK)] = product(REACH, at)

    chunks(centre)
    keep = pltpu.make_async_copy(part.at[0], middle, load_sem.at[4])
    keep.start()
    for pair in sent:
        for copy in pair:
            copy.wait_send()
    for copy in halos:
        copy.wait_send()
    keep.wait()
    for copy in sent[-1]:
        copy.wait_recv()


def chain(count, tab, p_blocks, a_blocks):
    anywhere = pl.BlockSpec(memory_space=pl.ANY)
    sums = [pltpu.VMEM((GROUP, width), BF16) for width in WIDTHS]
    return pl.pallas_call(
        functools.partial(chain_kernel, count),
        out_shape=(
            jax.ShapeDtypeStruct((GROUP, WIDE), BF16),
            jax.ShapeDtypeStruct((GROUP, WIDE), BF16),
            jax.ShapeDtypeStruct((GROUP, FRAME), BF16),
        ),
        in_specs=[pl.BlockSpec(memory_space=pltpu.SMEM), anywhere, anywhere],
        out_specs=[anywhere] * 3,
        scratch_shapes=[
            pltpu.VMEM((2, AGG, BS, KP * BS), BF16),
            pltpu.VMEM((NB, BS, KA * BS), BF16),
            pltpu.VMEM((2 * 14, ROWS, 128), BF16),
            pltpu.VMEM((2 * 4, ROWS, 128), BF16),
            pltpu.VMEM((2, ROWS, SLAB), BF16),
            pltpu.VMEM((5 * ROWS, FRAME), BF16),
            pltpu.VMEM((FRAME, 3 * ROWS), BF16),
            pltpu.VMEM((3 * ROWS, 3 * ROWS), BF16),
            pltpu.VMEM((3 * ROWS, FRAME), BF16),
            pltpu.VMEM((ROWS, FRAME), F32),
            pltpu.VMEM((2, GROUP, FRAME), BF16),
            *sums,
            *sums,
            pltpu.SemaphoreType.DMA((5,)),
            pltpu.SemaphoreType.DMA((2,)),
            pltpu.SemaphoreType.DMA((2,)),
            pltpu.SemaphoreType.DMA((REACH,)),
            pltpu.SemaphoreType.DMA((REACH,)),
            pltpu.SemaphoreType.DMA((REACH,)),
            pltpu.SemaphoreType.DMA((REACH,)),
        ],
        compiler_params=pltpu.CompilerParams(
            collective_id=0, has_side_effects=True, vmem_limit_bytes=63 * 2**20
        ),
    )(tab, p_blocks, a_blocks)


def gather_kernel(left_ref, right_ref, middle_ref, out_ref, tot):
    odd = lax.rem(lax.axis_index("dom"), 2)
    tot[:, :WIDE] = left_ref[...].astype(F32)
    tot[:, WIDE:] = jnp.zeros((BS, TOTAL - WIDE), F32)
    own = pl.ds(aligned((16 - 2 * odd) * BS), FRAME)
    tot[:, own] += middle_ref[...].astype(F32)
    tot[:, TOTAL - WIDE :] += right_ref[...].astype(F32)
    first = pl.program_id(0) + 1 - odd
    for start in range(NC + 1):

        @pl.when(first == start)
        def _():
            out_ref[0] = tot[:, start * BS : (start + BAND) * BS]


def gather(from_left, from_right, middle):
    return pl.pallas_call(
        gather_kernel,
        out_shape=jax.ShapeDtypeStruct((NC, BS, BAND * BS), F32),
        grid=(NC,),
        in_specs=[
            pl.BlockSpec((BS, WIDE), lambda i: (i, 0)),
            pl.BlockSpec((BS, WIDE), lambda i: (i, 0)),
            pl.BlockSpec((BS, FRAME), lambda i: (i, 0)),
        ],
        out_specs=pl.BlockSpec((1, BS, BAND * BS), lambda i: (i, 0, 0)),
        scratch_shapes=[pltpu.VMEM((BS, TOTAL), F32)],
    )(from_left, from_right, middle)


def body(a_blocks, p_blocks, cols_a, cols_p):
    count = lax.axis_size("dom")
    tab = tables(cols_a, cols_p, lax.axis_index("dom"), NC * count)
    return gather(*chain(count, tab, p_blocks, a_blocks))


def solution(mesh):
    in_specs = (P("dom", None, None), P("dom", None, None), P("dom", None), P("dom", None))
    out_specs = P("dom", None, None)
    return jax.shard_map(body, mesh=mesh, in_specs=in_specs, out_specs=out_specs, check_vma=False)
```

```python
import functools

import jax
import jax.numpy as jnp
from jax import lax
from jax.experimental import pallas as pl
from jax.experimental.pallas import tpu as pltpu
from jax.sharding import PartitionSpec as P

BS = 64
KA = 7
KP = 27
AGG = 8
H = 15
NC = 3
NB = 24
WIN = 31
BAND = 63
REACH = 5
MESH = pl.DeviceIdType.MESH

ROWS = AGG * BS
FRAME = 36 * BS
SLAB = 32 * BS
WIDE = 48 * BS
TOTAL = 66 * BS
FAR_WIDTH, FAR_SHIFT = [36, 38, 42, 44, 48], [0, 2, 6, 8, 12]
NEAR_WIDTH, NEAR_SHIFT = [36, 40, 42, 46, 48], [0, 4, 6, 10, 12]
GROUP = NC * BS
CHUNK = 768
F32 = jnp.float32
BF16 = jnp.bfloat16


def tables(cols_a, cols_p, device, count_agg):
    odd = device % 2
    agg_here = jnp.arange(NB, dtype=jnp.int32) // AGG
    slot = (cols_p - (device * NC + agg_here)[:, None] + H) % count_agg
    frame = slot + agg_here[:, None] + 1 + odd
    slab = slot + (1 - odd)
    target = jnp.concatenate([frame, slab[:AGG], slab[NB - AGG :]], axis=0)

    def tile_of(target, count, blocks, tiles):
        spots = jnp.arange(count, dtype=jnp.int32)
        order = jnp.arange(blocks, dtype=jnp.int32)
        hit = target[:, :, None] == spots[None, None, :]
        found = blocks + jnp.sum(jnp.where(hit, order[None, :, None] - blocks, 0), axis=1)
        return ((found ^ spots[None, :]) & 1) * tiles + (found >> 1)

    fine = (cols_a - ((device * NC + agg_here - 1) * AGG)[:, None]) % (count_agg * AGG)
    p_tile = tile_of(target, 36, KP, 14)
    a_tile = tile_of(fine, 24, KA, 4)
    return jnp.concatenate([p_tile, jnp.pad(a_tile, ((0, 0), (0, 12)))], axis=0)


def swap_halves(x):
    return jnp.concatenate([x[:, BS:], x[:, :BS]], axis=1)


def dot(a, b):
    return jnp.dot(a, b, preferred_element_type=F32)


def aligned(value, multiple=128):
    return pl.multiple_of(value, multiple)


def doubled(src, first, dst, wide, tiles):
    def step(e, _):
        rows = pl.ds(aligned(e * BS, BS), BS)
        for tile in range(tiles):
            if 128 * (tile + 1) <= wide:
                here = src[first + e, :, 128 * tile : 128 * tile + 128]
            else:
                here = jnp.concatenate([src[first + e, :, 128 * tile : wide], jnp.zeros((BS, BS), BF16)], axis=1)
            dst[tile, rows, :] = here
            dst[tiles + tile, rows, :] = swap_halves(here)
        return 0

    lax.fori_loop(0, AGG, step, 0)


def place(tab, first, src, dst, dst_row, pairs):
    low = lax.broadcasted_iota(jnp.int32, (BS, 128), 1) < BS

    def step(e, _):
        rows = pl.ds(aligned(e * BS, BS), BS)
        to = pl.ds(aligned(dst_row + e * BS, BS), BS)
        for pair in range(pairs):
            left = src[tab[first + e, 2 * pair], rows, :]
            right = src[tab[first + e, 2 * pair + 1], rows, :]
            dst[to, 128 * pair : 128 * pair + 128] = jnp.where(low, left, right)
        return 0

    lax.fori_loop(0, AGG, step, 0)


def chain_kernel(count, tab, p_blocks, a_blocks, from_far, from_near, middle, *scratch):
    raw, raw_a, p2, a2, slab, ext, pt, ad, w, wf, part = scratch[:11]
    to_far = [*scratch[11 : 11 + REACH], from_near]
    to_near = [*scratch[11 + REACH : 11 + 2 * REACH], from_far]
    load_sem, halo_send, halo_recv, send_far, recv_far, send_near, recv_near = scratch[11 + 2 * REACH :]
    me = lax.axis_index("dom")
    odd = lax.rem(me, 2)
    far, near = lax.rem(me + count - 1 + 2 * odd, count), lax.rem(me + count + 1 - 2 * odd, count)
    far_agg, near_agg = 2 * odd, 2 - 2 * odd

    def load(agg, slot, sem):
        return pltpu.make_async_copy(p_blocks.at[pl.ds(AGG * agg, AGG)], raw.at[slot], load_sem.at[sem])

    loads = [load(far_agg, 0, 0), load(near_agg, 1, 1)]
    load_a = pltpu.make_async_copy(a_blocks, raw_a, load_sem.at[2])
    for copy in (*loads, load_a):
        copy.start()
    barrier = pltpu.get_barrier_semaphore()
    for neighbour in (far, near):
        pl.semaphore_signal(barrier, inc=1, device_id=(neighbour,), device_id_type=MESH)

    def halo(side, target, edge):
        return pltpu.make_async_remote_copy(
            src_ref=slab.at[side],
            dst_ref=ext.at[pl.ds(aligned(edge * 4 * ROWS), ROWS), pl.ds(aligned(edge * 4 * BS), SLAB)],
            send_sem=halo_send.at[side],
            recv_sem=halo_recv.at[side],
            device_id=(target,),
            device_id_type=MESH,
        )

    halos = [halo(0, far, 1 - odd), halo(1, near, odd)]

    def own(agg):
        place(tab, AGG * agg, p2, ext, ROWS + ROWS * agg, 18)

    loads[0].wait()
    doubled(raw.at[0], 0, p2, KP * BS, 14)
    place(tab, NB + 4 * far_agg, p2, slab.at[0], 0, 16)
    pl.semaphore_wait(barrier, 2)
    halos[0].start()
    inner_load = load(1, 0, 3)
    inner_load.start()
    own(far_agg)
    loads[1].wait()
    doubled(raw.at[1], 0, p2, KP * BS, 14)
    place(tab, NB + 4 * near_agg, p2, slab.at[1], 0, 16)
    halos[1].start()
    own(near_agg)
    inner_load.wait()
    doubled(raw.at[0], 0, p2, KP * BS, 14)
    own(1)
    load_a.wait()
    for agg in range(NC):
        doubled(raw_a, AGG * agg, a2, KA * BS, 4)
        place(tab, NB + 2 * AGG + AGG * agg, a2, ad, ROWS * agg, 12)

    ext[:ROWS, SLAB:] = jnp.zeros((ROWS, FRAME - SLAB), BF16)
    ext[4 * ROWS :, : 4 * BS] = jnp.zeros((ROWS, 4 * BS), BF16)
    for step in range(1, REACH):
        for buf, more, goes_right, before in (
            (to_far, 2 * BS, odd, NEAR_WIDTH[step - 1]),
            (to_near, 4 * BS, 1 - odd, FAR_WIDTH[step - 1]),
        ):
            buf[step][:, pl.ds(aligned(goes_right * before * BS), more)] = jnp.zeros((GROUP, more), BF16)

    for agg in range(NC):

        def turn(tile, _):
            lanes = pl.ds(aligned(tile * 128), 128)
            pt[lanes, ROWS * agg : ROWS * (agg + 1)] = ext[ROWS * (agg + 1) : ROWS * (agg + 2), lanes].T
            return 0

        lax.fori_loop(0, FRAME // 128, turn, 0)

    def chunks(body):
        def step(n, _):
            body(aligned(n * CHUNK))
            return 0

        lax.fori_loop(0, FRAME // CHUNK, step, 0)

    far_rows = pl.ds(aligned(far_agg * ROWS), ROWS)
    near_rows = pl.ds(aligned(near_agg * ROWS), ROWS)

    def inner(at):
        cols = pl.ds(at, CHUNK)
        w[ROWS : 2 * ROWS, cols] = dot(ad[ROWS : 2 * ROWS, :], ext[ROWS : 4 * ROWS, cols]).astype(BF16)
        wf[:, cols] = dot(
            ad[far_rows, pl.ds(aligned(ROWS * (1 - odd)), 2 * ROWS)],
            ext[pl.ds(aligned(ROWS + ROWS * odd), 2 * ROWS), cols],
        )

    def near_side(at):
        cols = pl.ds(at, CHUNK)
        whole = dot(ad[near_rows, :], ext[pl.ds(aligned(2 * ROWS * (1 - odd)), 3 * ROWS), cols])
        w[near_rows, cols] = whole.astype(BF16)

    def far_side(at):
        cols = pl.ds(at, CHUNK)
        more = dot(
            ad[far_rows, pl.ds(aligned(2 * ROWS * odd), ROWS)],
            ext[pl.ds(aligned(4 * ROWS * odd), ROWS), cols],
        )
        w[far_rows, cols] = (wf[:, cols] + more).astype(BF16)

    chunks(inner)
    halos[1].wait_recv()
    chunks(near_side)
    halos[0].wait_recv()
    chunks(far_side)

    def product(group, at):
        rows = pl.ds(aligned((NC * group + 1 + odd) * BS, BS), GROUP)
        return dot(pt[rows, :], w[:, pl.ds(at, CHUNK)]).astype(BF16)

    def send(step, far_side):
        buf, lands = (to_far, to_near) if far_side else (to_near, to_far)
        width = (FAR_WIDTH if far_side else NEAR_WIDTH)[step] * BS
        grows = 0 if step == REACH - 1 else (4 * BS if far_side else 2 * BS)
        goes_left = 1 - odd if far_side else odd
        copy = pltpu.make_async_remote_copy(
            src_ref=buf[step],
            dst_ref=lands[step + 1].at[:, pl.ds(aligned(goes_left * grows), width)],
            send_sem=(send_far if far_side else send_near).at[step],
            recv_sem=(recv_far if far_side else recv_near).at[step],
            device_id=(far if far_side else near,),
            device_id_type=MESH,
        )
        copy.start()
        return copy

    def far_product(step, at):
        return product(REACH + (REACH - step) * (2 * odd - 1), at)

    def near_product(step, at):
        return product(REACH - (REACH - step) * (2 * odd - 1), at)

    def add(buf, shift, side):
        def some(at):
            cols = pl.ds(aligned(at + shift * BS), CHUNK)
            summed = buf[:, cols].astype(F32) + part[side, :, pl.ds(at, CHUNK)].astype(F32)
            buf[:, cols] = summed.astype(BF16)

        chunks(some)

    def far_first(at):
        to_far[0][:, pl.ds(at, CHUNK)] = far_product(0, at)

    def near_first(at):
        to_near[0][:, pl.ds(at, CHUNK)] = near_product(0, at)

    chunks(far_first)
    far_sent = [send(0, True)]
    chunks(near_first)
    near_sent = [send(0, False)]
    for step in range(REACH):

        def prepare(at):
            cols = pl.ds(at, CHUNK)
            if step > 0:
                part[1, :, cols] = near_product(step, at)
            if step + 1 < REACH:
                part[0, :, cols] = far_product(step + 1, at)

        chunks(prepare)
        if step > 0:
            far_sent[step - 1].wait_recv()
            add(to_near[step], NEAR_SHIFT[step] * (1 - odd), 1)
            near_sent.append(send(step, False))
        if step + 1 < REACH:
            near_sent[step].wait_recv()
            add(to_far[step + 1], FAR_SHIFT[step + 1] * odd, 0)
            far_sent.append(send(step + 1, True))

    def centre(at):
        part[0, :, pl.ds(at, CHUNK)] = product(REACH, at)

    chunks(centre)
    keep = pltpu.make_async_copy(part.at[0], middle, load_sem.at[4])
    keep.start()
    for copy in (*halos, *far_sent, *near_sent):
        copy.wait_send()
    keep.wait()
    near_sent[-1].wait_recv()
    far_sent[-1].wait_recv()


def chain(count, tab, p_blocks, a_blocks):
    anywhere = pl.BlockSpec(memory_space=pl.ANY)
    sums = [pltpu.VMEM((GROUP, width * BS), BF16) for width in (*FAR_WIDTH, *NEAR_WIDTH)]
    return pl.pallas_call(
        functools.partial(chain_kernel, count),
        out_shape=(
            jax.ShapeDtypeStruct((GROUP, WIDE), BF16),
            jax.ShapeDtypeStruct((GROUP, WIDE), BF16),
            jax.ShapeDtypeStruct((GROUP, FRAME), BF16),
        ),
        in_specs=[pl.BlockSpec(memory_space=pltpu.SMEM), anywhere, anywhere],
        out_specs=[anywhere] * 3,
        scratch_shapes=[
            pltpu.VMEM((2, AGG, BS, KP * BS), BF16),
            pltpu.VMEM((NB, BS, KA * BS), BF16),
            pltpu.VMEM((2 * 14, ROWS, 128), BF16),
            pltpu.VMEM((2 * 4, ROWS, 128), BF16),
            pltpu.VMEM((2, ROWS, SLAB), BF16),
            pltpu.VMEM((5 * ROWS, FRAME), BF16),
            pltpu.VMEM((FRAME, 3 * ROWS), BF16),
            pltpu.VMEM((3 * ROWS, 3 * ROWS), BF16),
            pltpu.VMEM((3 * ROWS, FRAME), BF16),
            pltpu.VMEM((ROWS, FRAME), F32),
            pltpu.VMEM((2, GROUP, FRAME), BF16),
            *sums,
            pltpu.SemaphoreType.DMA((5,)),
            pltpu.SemaphoreType.DMA((2,)),
            pltpu.SemaphoreType.DMA((2,)),
            pltpu.SemaphoreType.DMA((REACH,)),
            pltpu.SemaphoreType.DMA((REACH,)),
            pltpu.SemaphoreType.DMA((REACH,)),
            pltpu.SemaphoreType.DMA((REACH,)),
        ],
        compiler_params=pltpu.CompilerParams(
            collective_id=0, has_side_effects=True, vmem_limit_bytes=63 * 2**20
        ),
    )(tab, p_blocks, a_blocks)


def gather_kernel(far_ref, near_ref, middle_ref, out_ref, tot):
    odd = lax.rem(lax.axis_index("dom"), 2)
    tot[...] = jnp.zeros((BS, TOTAL), F32)
    for ref, start, width in (
        (far_ref, 18 * odd, WIDE),
        (near_ref, 18 * (1 - odd), WIDE),
        (middle_ref, 16 - 2 * odd, FRAME),
    ):
        tot[:, pl.ds(aligned(start * BS), width)] += ref[...].astype(F32)
    first = pl.program_id(0) + 1 - odd
    for start in range(NC + 1):

        @pl.when(first == start)
        def _():
            out_ref[0] = tot[:, start * BS : (start + BAND) * BS]


def gather(from_far, from_near, middle):
    return pl.pallas_call(
        gather_kernel,
        out_shape=jax.ShapeDtypeStruct((NC, BS, BAND * BS), F32),
        grid=(NC,),
        in_specs=[
            pl.BlockSpec((BS, WIDE), lambda i: (i, 0)),
            pl.BlockSpec((BS, WIDE), lambda i: (i, 0)),
            pl.BlockSpec((BS, FRAME), lambda i: (i, 0)),
        ],
        out_specs=pl.BlockSpec((1, BS, BAND * BS), lambda i: (i, 0, 0)),
        scratch_shapes=[pltpu.VMEM((BS, TOTAL), F32)],
    )(from_far, from_near, middle)


def body(a_blocks, p_blocks, cols_a, cols_p):
    count = lax.axis_size("dom")
    tab = tables(cols_a, cols_p, lax.axis_index("dom"), NC * count)
    return gather(*chain(count, tab, p_blocks, a_blocks))


def solution(mesh):
    in_specs = (P("dom", None, None), P("dom", None, None), P("dom", None), P("dom", None))
    out_specs = P("dom", None, None)
    return jax.shard_map(body, mesh=mesh, in_specs=in_specs, out_specs=out_specs, check_vma=False)
```

```python
import functools

import jax
import jax.numpy as jnp
from jax import lax
from jax.experimental import pallas as pl
from jax.experimental.pallas import tpu as pltpu
from jax.sharding import PartitionSpec as P

BS = 64
KA = 7
KP = 27
AGG = 8
H = 15
NC = 3
NB = 24
WIN = 31
BAND = 63
REACH = 5
MESH = pl.DeviceIdType.MESH

ROWS = AGG * BS
FRAME = 36 * BS
WIDE = 48 * BS
FAR_WIDTH, FAR_SHIFT = [36, 38, 42, 44, 48], [0, 2, 6, 8, 12]
NEAR_WIDTH, NEAR_SHIFT = [36, 40, 42, 46, 48], [0, 4, 6, 10, 12]
GROUP = NC * BS
PIECE = 2
CHUNK = 768
FIRST = FRAME // CHUNK
F32 = jnp.float32
BF16 = jnp.bfloat16


def tables(cols_a, cols_p, device, count_agg):
    odd = lax.rem(device, 2)

    def wrapped(x, period):
        x = jnp.where(x < 0, x + period, x)
        return jnp.where(x >= period, x - period, x)

    def tile_of(target, blocks, tiles):
        rows = target.shape[0]
        spots = lax.broadcasted_iota(jnp.int32, (rows, 128), 1)
        found = jnp.full((rows, 128), blocks, jnp.int32)
        for order in range(blocks):
            found = jnp.where(target[:, order : order + 1] == spots, order, found)
        return ((found ^ spots) & 1) * tiles + (found >> 1)

    agg = lax.broadcasted_iota(jnp.int32, (NB, KP), 0) >> 3
    slot = wrapped(cols_p - (device * NC + agg) + H, count_agg)
    agg_a = lax.broadcasted_iota(jnp.int32, (NB, KA), 0) >> 3
    fine = wrapped(cols_a - (device * NC + agg_a - 1) * AGG, count_agg * AGG)
    return (
        tile_of(slot + agg + 1 + odd, KP, 14),
        tile_of(slot[:AGG] + (5 - odd), KP, 14),
        tile_of(slot[NB - AGG :] + (1 - odd), KP, 14),
        tile_of(fine, KA, 4),
    )


def swap_halves(x):
    return jnp.concatenate([x[:, BS:], x[:, :BS]], axis=1)


def dot(a, b):
    return jnp.dot(a, b, preferred_element_type=F32)


def aligned(value, multiple=128):
    return pl.multiple_of(value, multiple)


def doubled(src, first, dst, wide, tiles, begin=0, end=AGG):
    def step(e, _):
        rows = pl.ds(aligned(e * BS, BS), BS)
        for tile in range(tiles):
            if 128 * (tile + 1) <= wide:
                here = src[first + e, :, 128 * tile : 128 * tile + 128]
            else:
                here = jnp.concatenate([src[first + e, :, 128 * tile : wide], jnp.zeros((BS, BS), BF16)], axis=1)
            dst[tile, rows, :] = here
            dst[tiles + tile, rows, :] = swap_halves(here)
        return 0

    lax.fori_loop(begin, end, step, 0)


def place(tab, first, src, dst, dst_row, pairs, begin=0, end=AGG):
    low = lax.broadcasted_iota(jnp.int32, (BS, 128), 1) < BS

    def step(e, _):
        rows = pl.ds(aligned(e * BS, BS), BS)
        to = pl.ds(aligned(dst_row + e * BS, BS), BS)
        for pair in range(pairs):
            left = src[tab[first + e, 2 * pair], rows, :]
            right = src[tab[first + e, 2 * pair + 1], rows, :]
            dst[to, 128 * pair : 128 * pair + 128] = jnp.where(low, left, right)
        return 0

    lax.fori_loop(begin, end, step, 0)


def chain_kernel(count, cols_a, cols_p, p_blocks, a_blocks, from_far, from_near, middle, *scratch):
    tab_made, tab, raw, raw_a, halo, halo_tab, tab_here, p2, a2, ext, pt, ad, w, wf, part = scratch[:15]
    to_far = [*scratch[15 : 15 + REACH], from_near]
    to_near = [*scratch[15 + REACH : 15 + 2 * REACH], from_far]
    load_sem, halo_send, halo_recv, send_far, recv_far, send_near, recv_near = scratch[15 + 2 * REACH :]
    me = lax.axis_index("dom")
    odd = lax.rem(me, 2)
    far, near = lax.rem(me + count - 1 + 2 * odd, count), lax.rem(me + count + 1 - 2 * odd, count)
    far_agg, near_agg = 2 * odd, 2 - 2 * odd

    def load(agg, slot, sem):
        return pltpu.make_async_copy(p_blocks.at[pl.ds(AGG * agg, AGG)], raw.at[slot], load_sem.at[sem])

    loads = [load(far_agg, 0, 0), load(near_agg, 1, 1)]
    load_a = pltpu.make_async_copy(a_blocks, raw_a, load_sem.at[2])
    for copy in (*loads, load_a):
        copy.start()
    barrier = pltpu.get_barrier_semaphore()
    for neighbour in (far, near):
        pl.semaphore_signal(barrier, inc=1, device_id=(neighbour,), device_id_type=MESH)

    def remote(src, dst, send_sem, recv_sem, target):
        return pltpu.make_async_remote_copy(
            src_ref=src, dst_ref=dst, send_sem=send_sem, recv_sem=recv_sem, device_id=(target,), device_id_type=MESH
        )

    def halo_copies(side, target, agg):
        copies = [
            remote(
                tab_made.at[pl.ds(aligned(NB + 4 * agg, 8), AGG)],
                halo_tab.at[side],
                halo_send.at[side, AGG // PIECE],
                halo_recv.at[side, AGG // PIECE],
                target,
            )
        ]
        for piece in range(AGG // PIECE):
            copies.append(
                remote(
                    p_blocks.at[pl.ds(AGG * agg + PIECE * piece, PIECE)],
                    halo.at[side, pl.ds(PIECE * piece, PIECE)],
                    halo_send.at[side, piece],
                    halo_recv.at[side, piece],
                    target,
                )
            )
        return copies

    halos = [halo_copies(0, far, far_agg), halo_copies(1, near, near_agg)]

    def own(agg):
        place(tab, AGG * agg, p2, ext, ROWS + ROWS * agg, 18)

    def arrived(side, edge):
        halos[side][0].wait_recv()
        pltpu.make_async_copy(halo_tab.at[side], tab_here.at[side], load_sem.at[5 + side]).start()
        pltpu.make_async_copy(halo_tab.at[side], tab_here.at[side], load_sem.at[5 + side]).wait()
        for piece in range(AGG // PIECE):
            rows = PIECE * piece, PIECE * (piece + 1)
            halos[side][1 + piece].wait_recv()
            doubled(halo.at[side], 0, p2, KP * BS, 14, *rows)
            place(tab_here.at[side], 0, p2, ext, 4 * ROWS * edge, 18, *rows)

    at = 0
    for made in tables(cols_a[...].T, cols_p[...], me, NC * count):
        tab_made[at : at + made.shape[0], :] = made
        at += made.shape[0]
    load_tab = pltpu.make_async_copy(tab_made, tab, load_sem.at[7])
    load_tab.start()
    loads[0].wait()
    doubled(raw.at[0], 0, p2, KP * BS, 14)
    inner_load = load(1, 0, 3)
    inner_load.start()
    pl.semaphore_wait(barrier, 2)
    for copy in (*halos[0], *halos[1]):
        copy.start()
    load_tab.wait()
    own(far_agg)
    loads[1].wait()
    doubled(raw.at[1], 0, p2, KP * BS, 14)
    own(near_agg)
    inner_load.wait()
    doubled(raw.at[0], 0, p2, KP * BS, 14)
    own(1)
    load_a.wait()
    for agg in range(NC):
        doubled(raw_a, AGG * agg, a2, KA * BS, 4)
        place(tab, NB + 2 * AGG + AGG * agg, a2, ad, ROWS * agg, 12)

    for step in range(1, REACH):
        for buf, more, goes_right, before in (
            (to_far, 2 * BS, odd, NEAR_WIDTH[step - 1]),
            (to_near, 4 * BS, 1 - odd, FAR_WIDTH[step - 1]),
        ):
            buf[step][:, pl.ds(aligned(goes_right * before * BS), more)] = jnp.zeros((GROUP, more), BF16)

    def turn(tile):
        lanes = pl.ds(aligned(tile * 128), 128)
        for agg in range(NC):
            pt[lanes, ROWS * agg : ROWS * (agg + 1)] = ext[ROWS * (agg + 1) : ROWS * (agg + 2), lanes].T

    def chunks(body):
        def step(n, _):
            body(aligned(n * CHUNK))
            return 0

        lax.fori_loop(0, FRAME // CHUNK, step, 0)

    far_rows = pl.ds(aligned(far_agg * ROWS), ROWS)
    near_rows = pl.ds(aligned(near_agg * ROWS), ROWS)

    def inner(at):
        cols = pl.ds(at, CHUNK)
        w[ROWS : 2 * ROWS, cols] = dot(ad[ROWS : 2 * ROWS, :], ext[ROWS : 4 * ROWS, cols]).astype(BF16)
        wf[:, cols] = dot(
            ad[far_rows, pl.ds(aligned(ROWS * (1 - odd)), 2 * ROWS)],
            ext[pl.ds(aligned(ROWS + ROWS * odd), 2 * ROWS), cols],
        )

    def near_side(at):
        cols = pl.ds(at, CHUNK)
        whole = dot(ad[near_rows, :], ext[pl.ds(aligned(2 * ROWS * (1 - odd)), 3 * ROWS), cols])
        w[near_rows, cols] = whole.astype(BF16)

    def far_side(at):
        cols = pl.ds(at, CHUNK)
        more = dot(
            ad[far_rows, pl.ds(aligned(2 * ROWS * odd), ROWS)],
            ext[pl.ds(aligned(4 * ROWS * odd), ROWS), cols],
        )
        w[far_rows, cols] = (wf[:, cols] + more).astype(BF16)

    def product(group, at):
        rows = pl.ds(aligned((NC * group + 1 + odd) * BS, BS), GROUP)
        return dot(pt[rows, :], w[:, pl.ds(at, CHUNK)]).astype(BF16)

    def send(step, far_side, at=0, width=None, sem=None):
        buf, lands = (to_far, to_near) if far_side else (to_near, to_far)
        width = (FAR_WIDTH if far_side else NEAR_WIDTH)[step] * BS if width is None else width
        sem = step + FIRST - 1 if sem is None else sem
        grows = 0 if step == REACH - 1 else (4 * BS if far_side else 2 * BS)
        goes_left = 1 - odd if far_side else odd
        copy = remote(
            buf[step].at[:, pl.ds(at, width)],
            lands[step + 1].at[:, pl.ds(aligned(goes_left * grows + at), width)],
            (send_far if far_side else send_near).at[sem],
            (recv_far if far_side else recv_near).at[sem],
            far if far_side else near,
        )
        copy.start()
        return [copy]

    def far_product(step, at):
        return product(REACH + (REACH - step) * (2 * odd - 1), at)

    def near_product(step, at):
        return product(REACH - (REACH - step) * (2 * odd - 1), at)

    def add(buf, shift, side):
        def some(at):
            cols = pl.ds(aligned(at + shift * BS), CHUNK)
            summed = buf[:, cols].astype(F32) + part[side, :, pl.ds(at, CHUNK)].astype(F32)
            buf[:, cols] = summed.astype(BF16)

        chunks(some)

    def far_first(at):
        to_far[0][:, pl.ds(at, CHUNK)] = far_product(0, at)

    def near_first(at):
        to_near[0][:, pl.ds(at, CHUNK)] = near_product(0, at)

    for tile in range(2):
        turn(tile + 16 * odd)
        turn(tile + 15 - 14 * odd)
        turn(tile + 2 + 12 * odd)
    arrived(1, 1 - odd)

    def ready(at):
        inner(at)
        near_side(at)

    def some_chunks(n, _):
        ready(aligned(n * CHUNK))
        return 0

    lax.fori_loop(0, FIRST - 1, some_chunks, 0)
    arrived(0, odd)
    far_sent, near_sent = [[]], [[]]
    for n in range(FIRST):
        at = n * CHUNK
        if n == FIRST - 1:
            ready(at)
        far_side(at)
        far_first(at)
        far_sent[0] += send(0, True, at, CHUNK, n)
        near_first(at)
        near_sent[0] += send(0, False, at, CHUNK, n)

    def turn_all(tile, _):
        turn(tile)
        return 0

    for step in range(REACH):
        if step == 1:
            lax.fori_loop(0, FRAME // 128, turn_all, 0)

        def prepare(at):
            cols = pl.ds(at, CHUNK)
            if step > 0:
                part[1, :, cols] = near_product(step, at)
            if step + 1 < REACH:
                part[0, :, cols] = far_product(step + 1, at)

        chunks(prepare)
        if step > 0:
            for copy in far_sent[step - 1]:
                copy.wait_recv()
            add(to_near[step], NEAR_SHIFT[step] * (1 - odd), 1)
            near_sent.append(send(step, False))
        if step + 1 < REACH:
            for copy in near_sent[step]:
                copy.wait_recv()
            add(to_far[step + 1], FAR_SHIFT[step + 1] * odd, 0)
            far_sent.append(send(step + 1, True))

    def centre(at):
        part[0, :, pl.ds(at, CHUNK)] = product(REACH, at)

    chunks(centre)
    keep = pltpu.make_async_copy(part.at[0], middle, load_sem.at[4])
    keep.start()
    for copies in (*halos, *far_sent, *near_sent):
        for copy in copies:
            copy.wait_send()
    keep.wait()
    near_sent[-1][0].wait_recv()
    far_sent[-1][0].wait_recv()


def chain(count, cols_a, cols_p, p_blocks, a_blocks):
    anywhere = pl.BlockSpec(memory_space=pl.ANY)
    sums = [pltpu.VMEM((GROUP, width * BS), BF16) for width in (*FAR_WIDTH, *NEAR_WIDTH)]
    return pl.pallas_call(
        functools.partial(chain_kernel, count),
        out_shape=(
            jax.ShapeDtypeStruct((GROUP, WIDE), BF16),
            jax.ShapeDtypeStruct((GROUP, WIDE), BF16),
            jax.ShapeDtypeStruct((GROUP, FRAME), BF16),
        ),
        in_specs=[pl.BlockSpec(memory_space=pltpu.VMEM), pl.BlockSpec(memory_space=pltpu.VMEM), anywhere, anywhere],
        out_specs=[anywhere] * 3,
        scratch_shapes=[
            pltpu.VMEM((2 * NB + 2 * AGG, 128), jnp.int32),
            pltpu.SMEM((2 * NB + 2 * AGG, 128), jnp.int32),
            pltpu.VMEM((2, AGG, BS, KP * BS), BF16),
            pltpu.VMEM((NB, BS, KA * BS), BF16),
            pltpu.VMEM((2, AGG, BS, KP * BS), BF16),
            pltpu.VMEM((2, AGG, 128), jnp.int32),
            pltpu.SMEM((2, AGG, 128), jnp.int32),
            pltpu.VMEM((2 * 14, ROWS, 128), BF16),
            pltpu.VMEM((2 * 4, ROWS, 128), BF16),
            pltpu.VMEM((5 * ROWS, FRAME), BF16),
            pltpu.VMEM((FRAME, 3 * ROWS), BF16),
            pltpu.VMEM((3 * ROWS, 3 * ROWS), BF16),
            pltpu.VMEM((3 * ROWS, FRAME), BF16),
            pltpu.VMEM((ROWS, FRAME), F32),
            pltpu.VMEM((2, GROUP, FRAME), BF16),
            *sums,
            pltpu.SemaphoreType.DMA((8,)),
            pltpu.SemaphoreType.DMA((2, AGG // PIECE + 1)),
            pltpu.SemaphoreType.DMA((2, AGG // PIECE + 1)),
            pltpu.SemaphoreType.DMA((REACH + FIRST - 1,)),
            pltpu.SemaphoreType.DMA((REACH + FIRST - 1,)),
            pltpu.SemaphoreType.DMA((REACH + FIRST - 1,)),
            pltpu.SemaphoreType.DMA((REACH + FIRST - 1,)),
        ],
        compiler_params=pltpu.CompilerParams(
            collective_id=0, has_side_effects=True, vmem_limit_bytes=63 * 2**20
        ),
    )(cols_a, cols_p, p_blocks, a_blocks)


def gather_kernel(far_ref, near_ref, middle_ref, out_ref):
    odd = lax.rem(lax.axis_index("dom"), 2)
    row = pl.program_id(0)

    def write(parity, first):
        parts = [
            (near_ref if parity else far_ref, 0, 48),
            (middle_ref, 16 - 2 * parity, 52 - 2 * parity),
            (far_ref if parity else near_ref, 18, 66),
        ]
        edges = sorted({edge for _, begin, end in parts for edge in (begin, end)})
        for begin, end in zip(edges[:-1], edges[1:]):
            terms = [
                ref[:, (begin - left) * BS : (end - left) * BS].astype(F32)
                for ref, left, right in parts
                if left <= begin and end <= right
            ]
            value = functools.reduce(jnp.add, terms)
            low, high = max(begin, first), min(end, first + BAND)
            out_ref[0, :, (low - first) * BS : (high - first) * BS] = value[:, (low - begin) * BS : (high - begin) * BS]

    for parity in (0, 1):
        for at in range(NC):

            @pl.when((odd == parity) & (row == at))
            def _():
                write(parity, at + 1 - parity)


def gather(from_far, from_near, middle):
    return pl.pallas_call(
        gather_kernel,
        out_shape=jax.ShapeDtypeStruct((NC, BS, BAND * BS), F32),
        grid=(NC,),
        in_specs=[
            pl.BlockSpec((BS, WIDE), lambda i: (i, 0)),
            pl.BlockSpec((BS, WIDE), lambda i: (i, 0)),
            pl.BlockSpec((BS, FRAME), lambda i: (i, 0)),
        ],
        out_specs=pl.BlockSpec((1, BS, BAND * BS), lambda i: (i, 0, 0)),
    )(from_far, from_near, middle)


def body(a_blocks, p_blocks, cols_a, cols_p):
    count = lax.axis_size("dom")
    return gather(*chain(count, cols_a.T, cols_p, p_blocks, a_blocks))


def solution(mesh):
    in_specs = (P("dom", None, None), P("dom", None, None), P("dom", None), P("dom", None))
    out_specs = P("dom", None, None)
    return jax.shard_map(body, mesh=mesh, in_specs=in_specs, out_specs=out_specs, check_vma=False)
```

```python
import functools

import jax
import jax.numpy as jnp
from jax import lax
from jax.experimental import pallas as pl
from jax.experimental.pallas import tpu as pltpu
from jax.sharding import PartitionSpec as P

BS = 64
KA = 7
KP = 27
AGG = 8
H = 15
NC = 3
NB = 24
WIN = 31
BAND = 63
REACH = 5
MESH = pl.DeviceIdType.MESH

ROWS = AGG * BS
FRAME = 36 * BS
WIDE = 48 * BS
FAR_WIDTH, FAR_SHIFT = [36, 38, 42, 44, 48], [0, 2, 6, 8, 12]
NEAR_WIDTH, NEAR_SHIFT = [36, 40, 42, 46, 48], [0, 4, 6, 10, 12]
GROUP = NC * BS
PIECE = 2
CHUNK = 768
FIRST = FRAME // CHUNK
F32 = jnp.float32
BF16 = jnp.bfloat16


def tables(cols_a, cols_p, device, count_agg):
    odd = lax.rem(device, 2)

    def wrapped(x, period):
        x = jnp.where(x < 0, x + period, x)
        return jnp.where(x >= period, x - period, x)

    def tile_of(target, blocks, tiles):
        rows = target.shape[0]
        spots = lax.broadcasted_iota(jnp.int32, (rows, 128), 1)
        found = jnp.full((rows, 128), blocks, jnp.int32)
        for order in range(blocks):
            found = jnp.where(target[:, order : order + 1] == spots, order, found)
        return ((found ^ spots) & 1) * tiles + (found >> 1)

    agg = lax.broadcasted_iota(jnp.int32, (NB, KP), 0) >> 3
    slot = wrapped(cols_p - (device * NC + agg) + H, count_agg)
    agg_a = lax.broadcasted_iota(jnp.int32, (NB, KA), 0) >> 3
    fine = wrapped(cols_a - (device * NC + agg_a - 1) * AGG, count_agg * AGG)
    return (
        tile_of(slot + agg + 1 + odd, KP, 14),
        tile_of(slot[:AGG] + (5 - odd), KP, 14),
        tile_of(slot[NB - AGG :] + (1 - odd), KP, 14),
        tile_of(fine, KA, 4),
    )


def swap_halves(x):
    return jnp.concatenate([x[:, BS:], x[:, :BS]], axis=1)


def dot(a, b):
    return jnp.dot(a, b, preferred_element_type=F32)


def aligned(value, multiple=128):
    return pl.multiple_of(value, multiple)


def doubled(src, first, dst, wide, tiles, begin=0, end=AGG):
    def step(e, _):
        rows = pl.ds(aligned(e * BS, BS), BS)
        for tile in range(tiles):
            if 128 * (tile + 1) <= wide:
                here = src[first + e, :, 128 * tile : 128 * tile + 128]
            else:
                here = jnp.concatenate([src[first + e, :, 128 * tile : wide], jnp.zeros((BS, BS), BF16)], axis=1)
            dst[tile, rows, :] = here
            dst[tiles + tile, rows, :] = swap_halves(here)
        return 0

    lax.fori_loop(begin, end, step, 0)


def place(tab, first, src, dst, dst_row, pairs, begin=0, end=AGG):
    low = lax.broadcasted_iota(jnp.int32, (BS, 128), 1) < BS

    def step(e, _):
        rows = pl.ds(aligned(e * BS, BS), BS)
        to = pl.ds(aligned(dst_row + e * BS, BS), BS)
        for pair in range(pairs):
            left = src[tab[first + e, 2 * pair], rows, :]
            right = src[tab[first + e, 2 * pair + 1], rows, :]
            dst[to, 128 * pair : 128 * pair + 128] = jnp.where(low, left, right)
        return 0

    lax.fori_loop(begin, end, step, 0)


def chain_kernel(count, cols_a, cols_p, p_blocks, a_blocks, from_far, from_near, middle, *scratch):
    tab_made, tab, raw, raw_a, halo, halo_tab, tab_here, p2, a2, ext, pt, ad, w, wf, part = scratch[:15]
    to_far = [*scratch[15 : 15 + REACH], from_near]
    to_near = [*scratch[15 + REACH : 15 + 2 * REACH], from_far]
    load_sem, halo_send, halo_recv, send_far, recv_far, send_near, recv_near = scratch[15 + 2 * REACH :]
    me = lax.axis_index("dom")
    odd = lax.rem(me, 2)
    far, near = lax.rem(me + count - 1 + 2 * odd, count), lax.rem(me + count + 1 - 2 * odd, count)
    far_agg, near_agg = 2 * odd, 2 - 2 * odd

    def load(agg, slot, sem):
        return pltpu.make_async_copy(p_blocks.at[pl.ds(AGG * agg, AGG)], raw.at[slot], load_sem.at[sem])

    loads = [load(far_agg, 0, 0), load(near_agg, 1, 1)]
    load_a = pltpu.make_async_copy(a_blocks, raw_a, load_sem.at[2])
    for copy in (*loads, load_a):
        copy.start()
    barrier = pltpu.get_barrier_semaphore()
    for neighbour in (far, near):
        pl.semaphore_signal(barrier, inc=1, device_id=(neighbour,), device_id_type=MESH)

    def remote(src, dst, send_sem, recv_sem, target):
        return pltpu.make_async_remote_copy(
            src_ref=src, dst_ref=dst, send_sem=send_sem, recv_sem=recv_sem, device_id=(target,), device_id_type=MESH
        )

    def halo_copies(side, target, agg):
        copies = [
            remote(
                tab_made.at[pl.ds(aligned(NB + 4 * agg, 8), AGG)],
                halo_tab.at[side],
                halo_send.at[side, AGG // PIECE],
                halo_recv.at[side, AGG // PIECE],
                target,
            )
        ]
        for piece in range(AGG // PIECE):
            copies.append(
                remote(
                    p_blocks.at[pl.ds(AGG * agg + PIECE * piece, PIECE)],
                    halo.at[side, pl.ds(PIECE * piece, PIECE)],
                    halo_send.at[side, piece],
                    halo_recv.at[side, piece],
                    target,
                )
            )
        return copies

    halos = [halo_copies(0, far, far_agg), halo_copies(1, near, near_agg)]

    def own(agg):
        place(tab, AGG * agg, p2, ext, ROWS + ROWS * agg, 18)

    def arrived(side, edge):
        halos[side][0].wait_recv()
        pltpu.make_async_copy(halo_tab.at[side], tab_here.at[side], load_sem.at[5 + side]).start()
        pltpu.make_async_copy(halo_tab.at[side], tab_here.at[side], load_sem.at[5 + side]).wait()
        for piece in range(AGG // PIECE):
            rows = PIECE * piece, PIECE * (piece + 1)
            halos[side][1 + piece].wait_recv()
            doubled(halo.at[side], 0, p2, KP * BS, 14, *rows)
            place(tab_here.at[side], 0, p2, ext, 4 * ROWS * edge, 18, *rows)

    at = 0
    for made in tables(cols_a[...].T, cols_p[...], me, NC * count):
        tab_made[at : at + made.shape[0], :] = made
        at += made.shape[0]
    load_tab = pltpu.make_async_copy(tab_made, tab, load_sem.at[7])
    load_tab.start()
    loads[0].wait()
    doubled(raw.at[0], 0, p2, KP * BS, 14)
    inner_load = load(1, 0, 3)
    inner_load.start()
    pl.semaphore_wait(barrier, 2)
    for copy in (*halos[0], *halos[1]):
        copy.start()
    load_tab.wait()
    own(far_agg)
    loads[1].wait()
    doubled(raw.at[1], 0, p2, KP * BS, 14)
    own(near_agg)
    inner_load.wait()
    doubled(raw.at[0], 0, p2, KP * BS, 14)
    own(1)
    load_a.wait()
    for agg in range(NC):
        doubled(raw_a, AGG * agg, a2, KA * BS, 4)
        place(tab, NB + 2 * AGG + AGG * agg, a2, ad, ROWS * agg, 12)

    for step in range(1, REACH):
        for buf, more, goes_right, before in (
            (to_far, 2 * BS, odd, NEAR_WIDTH[step - 1]),
            (to_near, 4 * BS, 1 - odd, FAR_WIDTH[step - 1]),
        ):
            buf[step][:, pl.ds(aligned(goes_right * before * BS), more)] = jnp.zeros((GROUP, more), BF16)

    def turn(tile):
        lanes = pl.ds(aligned(tile * 128), 128)
        for agg in range(NC):
            pt[lanes, ROWS * agg : ROWS * (agg + 1)] = ext[ROWS * (agg + 1) : ROWS * (agg + 2), lanes].T

    def chunks(body):
        def step(n, _):
            body(aligned(n * CHUNK))
            return 0

        lax.fori_loop(0, FRAME // CHUNK, step, 0)

    far_rows = pl.ds(aligned(far_agg * ROWS), ROWS)
    near_rows = pl.ds(aligned(near_agg * ROWS), ROWS)

    def inner(at):
        cols = pl.ds(at, CHUNK)
        w[ROWS : 2 * ROWS, cols] = dot(ad[ROWS : 2 * ROWS, :], ext[ROWS : 4 * ROWS, cols]).astype(BF16)
        wf[:, cols] = dot(
            ad[far_rows, pl.ds(aligned(ROWS * (1 - odd)), 2 * ROWS)],
            ext[pl.ds(aligned(ROWS + ROWS * odd), 2 * ROWS), cols],
        )

    def near_side(at):
        cols = pl.ds(at, CHUNK)
        whole = dot(ad[near_rows, :], ext[pl.ds(aligned(2 * ROWS * (1 - odd)), 3 * ROWS), cols])
        w[near_rows, cols] = whole.astype(BF16)

    def far_side(at):
        cols = pl.ds(at, CHUNK)
        more = dot(
            ad[far_rows, pl.ds(aligned(2 * ROWS * odd), ROWS)],
            ext[pl.ds(aligned(4 * ROWS * odd), ROWS), cols],
        )
        w[far_rows, cols] = (wf[:, cols] + more).astype(BF16)

    def product(group, at):
        rows = pl.ds(aligned((NC * group + 1 + odd) * BS, BS), GROUP)
        return dot(pt[rows, :], w[:, pl.ds(at, CHUNK)]).astype(BF16)

    def send(step, far_side, at=0, width=None, sem=None):
        buf, lands = (to_far, to_near) if far_side else (to_near, to_far)
        width = (FAR_WIDTH if far_side else NEAR_WIDTH)[step] * BS if width is None else width
        sem = step + FIRST - 1 if sem is None else sem
        grows = 0 if step == REACH - 1 else (4 * BS if far_side else 2 * BS)
        goes_left = 1 - odd if far_side else odd
        copy = remote(
            buf[step].at[:, pl.ds(at, width)],
            lands[step + 1].at[:, pl.ds(aligned(goes_left * grows + at), width)],
            (send_far if far_side else send_near).at[sem],
            (recv_far if far_side else recv_near).at[sem],
            far if far_side else near,
        )
        copy.start()
        return [copy]

    def far_product(step, at):
        return product(REACH + (REACH - step) * (2 * odd - 1), at)

    def near_product(step, at):
        return product(REACH - (REACH - step) * (2 * odd - 1), at)

    def add(buf, shift, side):
        def some(at):
            cols = pl.ds(aligned(at + shift * BS), CHUNK)
            summed = buf[:, cols].astype(F32) + part[side, :, pl.ds(at, CHUNK)].astype(F32)
            buf[:, cols] = summed.astype(BF16)

        chunks(some)

    def far_first(at):
        to_far[0][:, pl.ds(at, CHUNK)] = far_product(0, at)

    def near_first(at):
        to_near[0][:, pl.ds(at, CHUNK)] = near_product(0, at)

    for tile in range(2):
        turn(tile + 16 * odd)
        turn(tile + 15 - 14 * odd)
        turn(tile + 2 + 12 * odd)
    arrived(1, 1 - odd)

    def ready(at):
        inner(at)
        near_side(at)

    def some_chunks(n, _):
        ready(aligned(n * CHUNK))
        return 0

    lax.fori_loop(0, FIRST, some_chunks, 0)
    arrived(0, odd)
    far_sent, near_sent = [[]], [[]]
    for n in range(FIRST):
        at = n * CHUNK
        far_side(at)
        far_first(at)
        far_sent[0] += send(0, True, at, CHUNK, n)
        near_first(at)
        near_sent[0] += send(0, False, at, CHUNK, n)

    def turn_all(tile, _):
        turn(tile)
        return 0

    for step in range(REACH):
        if step == 1:
            lax.fori_loop(0, FRAME // 128, turn_all, 0)

        def prepare(at):
            cols = pl.ds(at, CHUNK)
            if step > 0:
                part[1, :, cols] = near_product(step, at)
            if step + 1 < REACH:
                part[0, :, cols] = far_product(step + 1, at)

        chunks(prepare)
        if step > 0:
            for copy in far_sent[step - 1]:
                copy.wait_recv()
            add(to_near[step], NEAR_SHIFT[step] * (1 - odd), 1)
            near_sent.append(send(step, False))
        if step + 1 < REACH:
            for copy in near_sent[step]:
                copy.wait_recv()
            add(to_far[step + 1], FAR_SHIFT[step + 1] * odd, 0)
            far_sent.append(send(step + 1, True))

    def centre(at):
        part[0, :, pl.ds(at, CHUNK)] = product(REACH, at)

    chunks(centre)
    keep = pltpu.make_async_copy(part.at[0], middle, load_sem.at[4])
    keep.start()
    for copies in (*halos, *far_sent, *near_sent):
        for copy in copies:
            copy.wait_send()
    keep.wait()
    near_sent[-1][0].wait_recv()
    far_sent[-1][0].wait_recv()


def chain(count, cols_a, cols_p, p_blocks, a_blocks):
    anywhere = pl.BlockSpec(memory_space=pl.ANY)
    sums = [pltpu.VMEM((GROUP, width * BS), BF16) for width in (*FAR_WIDTH, *NEAR_WIDTH)]
    return pl.pallas_call(
        functools.partial(chain_kernel, count),
        out_shape=(
            jax.ShapeDtypeStruct((GROUP, WIDE), BF16),
            jax.ShapeDtypeStruct((GROUP, WIDE), BF16),
            jax.ShapeDtypeStruct((GROUP, FRAME), BF16),
        ),
        in_specs=[pl.BlockSpec(memory_space=pltpu.VMEM), pl.BlockSpec(memory_space=pltpu.VMEM), anywhere, anywhere],
        out_specs=[anywhere] * 3,
        scratch_shapes=[
            pltpu.VMEM((2 * NB + 2 * AGG, 128), jnp.int32),
            pltpu.SMEM((2 * NB + 2 * AGG, 128), jnp.int32),
            pltpu.VMEM((2, AGG, BS, KP * BS), BF16),
            pltpu.VMEM((NB, BS, KA * BS), BF16),
            pltpu.VMEM((2, AGG, BS, KP * BS), BF16),
            pltpu.VMEM((2, AGG, 128), jnp.int32),
            pltpu.SMEM((2, AGG, 128), jnp.int32),
            pltpu.VMEM((2 * 14, ROWS, 128), BF16),
            pltpu.VMEM((2 * 4, ROWS, 128), BF16),
            pltpu.VMEM((5 * ROWS, FRAME), BF16),
            pltpu.VMEM((FRAME, 3 * ROWS), BF16),
            pltpu.VMEM((3 * ROWS, 3 * ROWS), BF16),
            pltpu.VMEM((3 * ROWS, FRAME), BF16),
            pltpu.VMEM((ROWS, FRAME), F32),
            pltpu.VMEM((2, GROUP, FRAME), BF16),
            *sums,
            pltpu.SemaphoreType.DMA((8,)),
            pltpu.SemaphoreType.DMA((2, AGG // PIECE + 1)),
            pltpu.SemaphoreType.DMA((2, AGG // PIECE + 1)),
            pltpu.SemaphoreType.DMA((REACH + FIRST - 1,)),
            pltpu.SemaphoreType.DMA((REACH + FIRST - 1,)),
            pltpu.SemaphoreType.DMA((REACH + FIRST - 1,)),
            pltpu.SemaphoreType.DMA((REACH + FIRST - 1,)),
        ],
        compiler_params=pltpu.CompilerParams(
            collective_id=0, has_side_effects=True, vmem_limit_bytes=63 * 2**20
        ),
    )(cols_a, cols_p, p_blocks, a_blocks)


def gather_kernel(from_far, from_near, middle, out, far_ref, near_ref, middle_ref, out_ref, load_sem, store_sem):
    odd = lax.rem(lax.axis_index("dom"), 2)
    pairs = ((from_far, far_ref), (from_near, near_ref), (middle, middle_ref))
    loads = [
        [
            pltpu.make_async_copy(src.at[pl.ds(BS * row, BS)], dst.at[row], load_sem.at[row, kind])
            for kind, (src, dst) in enumerate(pairs)
        ]
        for row in range(NC)
    ]
    stores = [pltpu.make_async_copy(out_ref.at[row], out.at[row], store_sem.at[row]) for row in range(NC)]
    for copies in loads:
        for copy in copies:
            copy.start()

    def write(row, parity):
        first = row + 1 - parity
        parts = [
            (near_ref if parity else far_ref, 0, 48),
            (middle_ref, 16 - 2 * parity, 52 - 2 * parity),
            (far_ref if parity else near_ref, 18, 66),
        ]
        edges = sorted({edge for _, begin, end in parts for edge in (begin, end)})
        for begin, end in zip(edges[:-1], edges[1:]):
            terms = [
                ref[row, :, (begin - left) * BS : (end - left) * BS].astype(F32)
                for ref, left, right in parts
                if left <= begin and end <= right
            ]
            value = functools.reduce(jnp.add, terms)
            low, high = max(begin, first), min(end, first + BAND)
            out_ref[row, :, (low - first) * BS : (high - first) * BS] = value[:, (low - begin) * BS : (high - begin) * BS]

    for row in range(NC):
        for copy in loads[row]:
            copy.wait()
        for parity in (0, 1):
            pl.when(odd == parity)(functools.partial(write, row, parity))
        stores[row].start()
    for copy in stores:
        copy.wait()


def gather(from_far, from_near, middle):
    anywhere = pl.BlockSpec(memory_space=pl.ANY)
    return pl.pallas_call(
        gather_kernel,
        out_shape=jax.ShapeDtypeStruct((NC, BS, BAND * BS), F32),
        in_specs=[anywhere] * 3,
        out_specs=anywhere,
        scratch_shapes=[
            pltpu.VMEM((NC, BS, WIDE), BF16),
            pltpu.VMEM((NC, BS, WIDE), BF16),
            pltpu.VMEM((NC, BS, FRAME), BF16),
            pltpu.VMEM((NC, BS, BAND * BS), F32),
            pltpu.SemaphoreType.DMA((NC, 3)),
            pltpu.SemaphoreType.DMA((NC,)),
        ],
        compiler_params=pltpu.CompilerParams(vmem_limit_bytes=62 * 2**20),
    )(from_far, from_near, middle)


def body(a_blocks, p_blocks, cols_a, cols_p):
    count = lax.axis_size("dom")
    return gather(*chain(count, cols_a.T, cols_p, p_blocks, a_blocks))


def solution(mesh):
    in_specs = (P("dom", None, None), P("dom", None, None), P("dom", None), P("dom", None))
    out_specs = P("dom", None, None)
    return jax.shard_map(body, mesh=mesh, in_specs=in_specs, out_specs=out_specs, check_vma=False)
```

```python
import functools

import jax
import jax.numpy as jnp
from jax import lax
from jax.experimental import pallas as pl
from jax.experimental.pallas import tpu as pltpu
from jax.sharding import PartitionSpec as P

BS = 64
KA = 7
KP = 27
AGG = 8
H = 15
NC = 3
NB = 24
WIN = 31
BAND = 63
REACH = 5
MESH = pl.DeviceIdType.MESH

ROWS = AGG * BS
FRAME = 36 * BS
WIDE = 48 * BS
FAR_WIDTH, FAR_SHIFT = [36, 38, 42, 44, 48], [0, 2, 6, 8, 12]
NEAR_WIDTH, NEAR_SHIFT = [36, 40, 42, 46, 48], [0, 4, 6, 10, 12]
GROUP = NC * BS
PIECE = 2
CHUNK = 768
FIRST = FRAME // CHUNK
F32 = jnp.float32
BF16 = jnp.bfloat16


def tables(cols_a, cols_p, device, count_agg):
    odd = lax.rem(device, 2)

    def wrapped(x, period):
        x = jnp.where(x < 0, x + period, x)
        return jnp.where(x >= period, x - period, x)

    def tile_of(target, blocks, tiles):
        rows = target.shape[0]
        spots = lax.broadcasted_iota(jnp.int32, (rows, 128), 1)
        found = jnp.full((rows, 128), blocks, jnp.int32)
        for order in range(blocks):
            found = jnp.where(target[:, order : order + 1] == spots, order, found)
        return ((found ^ spots) & 1) * tiles + (found >> 1)

    agg = lax.broadcasted_iota(jnp.int32, (NB, KP), 0) >> 3
    slot = wrapped(cols_p - (device * NC + agg) + H, count_agg)
    agg_a = lax.broadcasted_iota(jnp.int32, (NB, KA), 0) >> 3
    fine = wrapped(cols_a - (device * NC + agg_a - 1) * AGG, count_agg * AGG)
    return (
        tile_of(slot + agg + 1 + odd, KP, 14),
        tile_of(slot[:AGG] + (5 - odd), KP, 14),
        tile_of(slot[NB - AGG :] + (1 - odd), KP, 14),
        tile_of(fine, KA, 4),
    )


def swap_halves(x):
    return jnp.concatenate([x[:, BS:], x[:, :BS]], axis=1)


def dot(a, b):
    return jnp.dot(a, b, preferred_element_type=F32)


def aligned(value, multiple=128):
    return pl.multiple_of(value, multiple)


def doubled(src, first, dst, wide, tiles, begin=0, end=AGG):
    def step(e, _):
        rows = pl.ds(aligned(e * BS, BS), BS)
        for tile in range(tiles):
            if 128 * (tile + 1) <= wide:
                here = src[first + e, :, 128 * tile : 128 * tile + 128]
            else:
                here = jnp.concatenate([src[first + e, :, 128 * tile : wide], jnp.zeros((BS, BS), BF16)], axis=1)
            dst[tile, rows, :] = here
            dst[tiles + tile, rows, :] = swap_halves(here)
        return 0

    lax.fori_loop(begin, end, step, 0)


def place(tab, first, src, dst, dst_row, pairs, begin=0, end=AGG):
    low = lax.broadcasted_iota(jnp.int32, (BS, 128), 1) < BS

    def step(e, _):
        rows = pl.ds(aligned(e * BS, BS), BS)
        to = pl.ds(aligned(dst_row + e * BS, BS), BS)
        for pair in range(pairs):
            left = src[tab[first + e, 2 * pair], rows, :]
            right = src[tab[first + e, 2 * pair + 1], rows, :]
            dst[to, 128 * pair : 128 * pair + 128] = jnp.where(low, left, right)
        return 0

    lax.fori_loop(begin, end, step, 0)


def chain_kernel(count, cols_a, cols_p, p_blocks, a_blocks, from_far, from_near, middle, *scratch):
    here_a, here_p, tab_made, tab, raw, raw_a, halo, halo_tab, tab_here, p2, a2, ext, pt, ad, w, wf, part = scratch[:17]
    to_far = [*scratch[17 : 17 + REACH], from_near]
    to_near = [*scratch[17 + REACH : 17 + 2 * REACH], from_far]
    load_sem, halo_send, halo_recv, send_far, recv_far, send_near, recv_near = scratch[17 + 2 * REACH :]
    me = lax.axis_index("dom")
    odd = lax.rem(me, 2)
    far, near = lax.rem(me + count - 1 + 2 * odd, count), lax.rem(me + count + 1 - 2 * odd, count)
    far_agg, near_agg = 2 * odd, 2 - 2 * odd

    def load(agg, slot, sem):
        return pltpu.make_async_copy(p_blocks.at[pl.ds(AGG * agg, AGG)], raw.at[slot], load_sem.at[sem])

    barrier = pltpu.get_barrier_semaphore()
    for neighbour in (far, near):
        pl.semaphore_signal(barrier, inc=1, device_id=(neighbour,), device_id_type=MESH)
    load_cols = [
        pltpu.make_async_copy(cols_a, here_a, load_sem.at[8]),
        pltpu.make_async_copy(cols_p, here_p, load_sem.at[9]),
    ]
    loads = [load(far_agg, 0, 0), load(near_agg, 1, 1)]
    load_a = pltpu.make_async_copy(a_blocks, raw_a, load_sem.at[2])
    for copy in (*load_cols, *loads, load_a):
        copy.start()

    def remote(src, dst, send_sem, recv_sem, target):
        return pltpu.make_async_remote_copy(
            src_ref=src, dst_ref=dst, send_sem=send_sem, recv_sem=recv_sem, device_id=(target,), device_id_type=MESH
        )

    def halo_copies(side, target, agg):
        copies = [
            remote(
                tab_made.at[pl.ds(aligned(NB + 4 * agg, 8), AGG)],
                halo_tab.at[side],
                halo_send.at[side, AGG // PIECE],
                halo_recv.at[side, AGG // PIECE],
                target,
            )
        ]
        for piece in range(AGG // PIECE):
            copies.append(
                remote(
                    p_blocks.at[pl.ds(AGG * agg + PIECE * piece, PIECE)],
                    halo.at[side, pl.ds(PIECE * piece, PIECE)],
                    halo_send.at[side, piece],
                    halo_recv.at[side, piece],
                    target,
                )
            )
        return copies

    halos = [halo_copies(0, far, far_agg), halo_copies(1, near, near_agg)]

    def own(agg):
        place(tab, AGG * agg, p2, ext, ROWS + ROWS * agg, 18)

    def arrived(side, edge):
        halos[side][0].wait_recv()
        pltpu.make_async_copy(halo_tab.at[side], tab_here.at[side], load_sem.at[5 + side]).start()
        pltpu.make_async_copy(halo_tab.at[side], tab_here.at[side], load_sem.at[5 + side]).wait()
        for piece in range(AGG // PIECE):
            rows = PIECE * piece, PIECE * (piece + 1)
            halos[side][1 + piece].wait_recv()
            doubled(halo.at[side], 0, p2, KP * BS, 14, *rows)
            place(tab_here.at[side], 0, p2, ext, 4 * ROWS * edge, 18, *rows)

    for copy in load_cols:
        copy.wait()
    at = 0
    for made in tables(here_a[...].T, here_p[...], me, NC * count):
        tab_made[at : at + made.shape[0], :] = made
        at += made.shape[0]
    load_tab = pltpu.make_async_copy(tab_made, tab, load_sem.at[7])
    load_tab.start()
    loads[0].wait()
    doubled(raw.at[0], 0, p2, KP * BS, 14)
    inner_load = load(1, 0, 3)
    inner_load.start()
    pl.semaphore_wait(barrier, 2)
    for copy in (*halos[0], *halos[1]):
        copy.start()
    load_tab.wait()
    own(far_agg)
    loads[1].wait()
    doubled(raw.at[1], 0, p2, KP * BS, 14)
    own(near_agg)
    inner_load.wait()
    doubled(raw.at[0], 0, p2, KP * BS, 14)
    own(1)
    load_a.wait()
    for agg in range(NC):
        doubled(raw_a, AGG * agg, a2, KA * BS, 4)
        place(tab, NB + 2 * AGG + AGG * agg, a2, ad, ROWS * agg, 12)

    for step in range(1, REACH):
        for buf, more, goes_right, before in (
            (to_far, 2 * BS, odd, NEAR_WIDTH[step - 1]),
            (to_near, 4 * BS, 1 - odd, FAR_WIDTH[step - 1]),
        ):
            buf[step][:, pl.ds(aligned(goes_right * before * BS), more)] = jnp.zeros((GROUP, more), BF16)

    def turn(tile):
        lanes = pl.ds(aligned(tile * 128), 128)
        for agg in range(NC):
            pt[lanes, ROWS * agg : ROWS * (agg + 1)] = ext[ROWS * (agg + 1) : ROWS * (agg + 2), lanes].T

    def chunks(body):
        def step(n, _):
            body(aligned(n * CHUNK))
            return 0

        lax.fori_loop(0, FRAME // CHUNK, step, 0)

    far_rows = pl.ds(aligned(far_agg * ROWS), ROWS)
    near_rows = pl.ds(aligned(near_agg * ROWS), ROWS)

    def inner(at):
        cols = pl.ds(at, CHUNK)
        w[ROWS : 2 * ROWS, cols] = dot(ad[ROWS : 2 * ROWS, :], ext[ROWS : 4 * ROWS, cols]).astype(BF16)
        wf[:, cols] = dot(
            ad[far_rows, pl.ds(aligned(ROWS * (1 - odd)), 2 * ROWS)],
            ext[pl.ds(aligned(ROWS + ROWS * odd), 2 * ROWS), cols],
        )

    def near_side(at):
        cols = pl.ds(at, CHUNK)
        whole = dot(ad[near_rows, :], ext[pl.ds(aligned(2 * ROWS * (1 - odd)), 3 * ROWS), cols])
        w[near_rows, cols] = whole.astype(BF16)

    def far_side(at):
        cols = pl.ds(at, CHUNK)
        more = dot(
            ad[far_rows, pl.ds(aligned(2 * ROWS * odd), ROWS)],
            ext[pl.ds(aligned(4 * ROWS * odd), ROWS), cols],
        )
        w[far_rows, cols] = (wf[:, cols] + more).astype(BF16)

    def product(group, at):
        rows = pl.ds(aligned((NC * group + 1 + odd) * BS, BS), GROUP)
        return dot(pt[rows, :], w[:, pl.ds(at, CHUNK)]).astype(BF16)

    def send(step, far_side, at=0, width=None, sem=None):
        buf, lands = (to_far, to_near) if far_side else (to_near, to_far)
        width = (FAR_WIDTH if far_side else NEAR_WIDTH)[step] * BS if width is None else width
        sem = step + FIRST - 1 if sem is None else sem
        grows = 0 if step == REACH - 1 else (4 * BS if far_side else 2 * BS)
        goes_left = 1 - odd if far_side else odd
        copy = remote(
            buf[step].at[:, pl.ds(at, width)],
            lands[step + 1].at[:, pl.ds(aligned(goes_left * grows + at), width)],
            (send_far if far_side else send_near).at[sem],
            (recv_far if far_side else recv_near).at[sem],
            far if far_side else near,
        )
        copy.start()
        return [copy]

    def far_product(step, at):
        return product(REACH + (REACH - step) * (2 * odd - 1), at)

    def near_product(step, at):
        return product(REACH - (REACH - step) * (2 * odd - 1), at)

    def add(buf, shift, side):
        def some(at):
            cols = pl.ds(aligned(at + shift * BS), CHUNK)
            summed = buf[:, cols].astype(F32) + part[side, :, pl.ds(at, CHUNK)].astype(F32)
            buf[:, cols] = summed.astype(BF16)

        chunks(some)

    def far_first(at):
        to_far[0][:, pl.ds(at, CHUNK)] = far_product(0, at)

    def near_first(at):
        to_near[0][:, pl.ds(at, CHUNK)] = near_product(0, at)

    for tile in range(2):
        turn(tile + 16 * odd)
        turn(tile + 15 - 14 * odd)
        turn(tile + 2 + 12 * odd)
    arrived(1, 1 - odd)

    def ready(at):
        inner(at)
        near_side(at)

    def some_chunks(n, _):
        ready(aligned(n * CHUNK))
        return 0

    lax.fori_loop(0, FIRST, some_chunks, 0)
    arrived(0, odd)
    far_sent, near_sent = [[]], [[]]
    for n in range(FIRST):
        at = n * CHUNK
        far_side(at)
        far_first(at)
        far_sent[0] += send(0, True, at, CHUNK, n)
        near_first(at)
        near_sent[0] += send(0, False, at, CHUNK, n)

    def turn_all(tile, _):
        turn(tile)
        return 0

    for step in range(REACH):
        if step == 1:
            lax.fori_loop(0, FRAME // 128, turn_all, 0)

        def prepare(at):
            cols = pl.ds(at, CHUNK)
            if step > 0:
                part[1, :, cols] = near_product(step, at)
            if step + 1 < REACH:
                part[0, :, cols] = far_product(step + 1, at)

        chunks(prepare)
        if step > 0:
            for copy in far_sent[step - 1]:
                copy.wait_recv()
            add(to_near[step], NEAR_SHIFT[step] * (1 - odd), 1)
            near_sent.append(send(step, False))
        if step + 1 < REACH:
            for copy in near_sent[step]:
                copy.wait_recv()
            add(to_far[step + 1], FAR_SHIFT[step + 1] * odd, 0)
            far_sent.append(send(step + 1, True))

    def centre(at):
        part[0, :, pl.ds(at, CHUNK)] = product(REACH, at)

    chunks(centre)
    keep = pltpu.make_async_copy(part.at[0], middle, load_sem.at[4])
    keep.start()
    for copies in (*halos, *far_sent, *near_sent):
        for copy in copies:
            copy.wait_send()
    keep.wait()
    near_sent[-1][0].wait_recv()
    far_sent[-1][0].wait_recv()


def chain(count, cols_a, cols_p, p_blocks, a_blocks):
    anywhere = pl.BlockSpec(memory_space=pl.ANY)
    sums = [pltpu.VMEM((GROUP, width * BS), BF16) for width in (*FAR_WIDTH, *NEAR_WIDTH)]
    return pl.pallas_call(
        functools.partial(chain_kernel, count),
        out_shape=(
            jax.ShapeDtypeStruct((GROUP, WIDE), BF16),
            jax.ShapeDtypeStruct((GROUP, WIDE), BF16),
            jax.ShapeDtypeStruct((GROUP, FRAME), BF16),
        ),
        in_specs=[anywhere] * 4,
        out_specs=[anywhere] * 3,
        scratch_shapes=[
            pltpu.VMEM((KA, NB), jnp.int32),
            pltpu.VMEM((NB, KP), jnp.int32),
            pltpu.VMEM((2 * NB + 2 * AGG, 128), jnp.int32),
            pltpu.SMEM((2 * NB + 2 * AGG, 128), jnp.int32),
            pltpu.VMEM((2, AGG, BS, KP * BS), BF16),
            pltpu.VMEM((NB, BS, KA * BS), BF16),
            pltpu.VMEM((2, AGG, BS, KP * BS), BF16),
            pltpu.VMEM((2, AGG, 128), jnp.int32),
            pltpu.SMEM((2, AGG, 128), jnp.int32),
            pltpu.VMEM((2 * 14, ROWS, 128), BF16),
            pltpu.VMEM((2 * 4, ROWS, 128), BF16),
            pltpu.VMEM((5 * ROWS, FRAME), BF16),
            pltpu.VMEM((FRAME, 3 * ROWS), BF16),
            pltpu.VMEM((3 * ROWS, 3 * ROWS), BF16),
            pltpu.VMEM((3 * ROWS, FRAME), BF16),
            pltpu.VMEM((ROWS, FRAME), F32),
            pltpu.VMEM((2, GROUP, FRAME), BF16),
            *sums,
            pltpu.SemaphoreType.DMA((10,)),
            pltpu.SemaphoreType.DMA((2, AGG // PIECE + 1)),
            pltpu.SemaphoreType.DMA((2, AGG // PIECE + 1)),
            pltpu.SemaphoreType.DMA((REACH + FIRST - 1,)),
            pltpu.SemaphoreType.DMA((REACH + FIRST - 1,)),
            pltpu.SemaphoreType.DMA((REACH + FIRST - 1,)),
            pltpu.SemaphoreType.DMA((REACH + FIRST - 1,)),
        ],
        compiler_params=pltpu.CompilerParams(
            collective_id=0, has_side_effects=True, vmem_limit_bytes=63 * 2**20
        ),
    )(cols_a, cols_p, p_blocks, a_blocks)


def gather_kernel(from_far, from_near, middle, out, far_ref, near_ref, middle_ref, out_ref, load_sem, store_sem):
    odd = lax.rem(lax.axis_index("dom"), 2)
    pairs = ((from_far, far_ref), (from_near, near_ref), (middle, middle_ref))
    loads = [
        [
            pltpu.make_async_copy(src.at[pl.ds(BS * row, BS)], dst.at[row], load_sem.at[row, kind])
            for kind, (src, dst) in enumerate(pairs)
        ]
        for row in range(NC)
    ]
    stores = [pltpu.make_async_copy(out_ref.at[row], out.at[row], store_sem.at[row]) for row in range(NC)]
    for copies in loads:
        for copy in copies:
            copy.start()

    def write(row, parity):
        first = row + 1 - parity
        parts = [
            (near_ref if parity else far_ref, 0, 48),
            (middle_ref, 16 - 2 * parity, 52 - 2 * parity),
            (far_ref if parity else near_ref, 18, 66),
        ]
        edges = sorted({edge for _, begin, end in parts for edge in (begin, end)})
        for begin, end in zip(edges[:-1], edges[1:]):
            terms = [
                ref[row, :, (begin - left) * BS : (end - left) * BS].astype(F32)
                for ref, left, right in parts
                if left <= begin and end <= right
            ]
            value = functools.reduce(jnp.add, terms)
            low, high = max(begin, first), min(end, first + BAND)
            out_ref[row, :, (low - first) * BS : (high - first) * BS] = value[:, (low - begin) * BS : (high - begin) * BS]

    for row in range(NC):
        for copy in loads[row]:
            copy.wait()
        for parity in (0, 1):
            pl.when(odd == parity)(functools.partial(write, row, parity))
        stores[row].start()
    for copy in stores:
        copy.wait()


def gather(from_far, from_near, middle):
    anywhere = pl.BlockSpec(memory_space=pl.ANY)
    return pl.pallas_call(
        gather_kernel,
        out_shape=jax.ShapeDtypeStruct((NC, BS, BAND * BS), F32),
        in_specs=[anywhere] * 3,
        out_specs=anywhere,
        scratch_shapes=[
            pltpu.VMEM((NC, BS, WIDE), BF16),
            pltpu.VMEM((NC, BS, WIDE), BF16),
            pltpu.VMEM((NC, BS, FRAME), BF16),
            pltpu.VMEM((NC, BS, BAND * BS), F32),
            pltpu.SemaphoreType.DMA((NC, 3)),
            pltpu.SemaphoreType.DMA((NC,)),
        ],
        compiler_params=pltpu.CompilerParams(vmem_limit_bytes=62 * 2**20),
    )(from_far, from_near, middle)


def body(a_blocks, p_blocks, cols_a, cols_p):
    count = lax.axis_size("dom")
    return gather(*chain(count, cols_a.T, cols_p, p_blocks, a_blocks))


def solution(mesh):
    in_specs = (P("dom", None, None), P("dom", None, None), P("dom", None), P("dom", None))
    out_specs = P("dom", None, None)
    return jax.shard_map(body, mesh=mesh, in_specs=in_specs, out_specs=out_specs, check_vma=False)
```

```python
import functools

import jax
import jax.numpy as jnp
from jax import lax
from jax.experimental import pallas as pl
from jax.experimental.pallas import tpu as pltpu
from jax.sharding import PartitionSpec as P

BS = 64
KA = 7
KP = 27
AGG = 8
H = 15
NC = 3
NB = 24
WIN = 31
BAND = 63
REACH = 5
MESH = pl.DeviceIdType.MESH

ROWS = AGG * BS
FRAME = 36 * BS
WIDE = 48 * BS
FAR_WIDTH, FAR_SHIFT = [36, 38, 42, 44, 48], [0, 2, 6, 8, 12]
NEAR_WIDTH, NEAR_SHIFT = [36, 40, 42, 46, 48], [0, 4, 6, 10, 12]
GROUP = NC * BS
PIECE = 1
CHUNK = 768
FIRST = FRAME // CHUNK
F32 = jnp.float32
BF16 = jnp.bfloat16


def tables(cols_a, cols_p, device, count_agg):
    odd = lax.rem(device, 2)

    def wrapped(x, period):
        x = jnp.where(x < 0, x + period, x)
        return jnp.where(x >= period, x - period, x)

    def tile_of(target, blocks, tiles):
        rows = target.shape[0]
        spots = lax.broadcasted_iota(jnp.int32, (rows, 128), 1)
        found = jnp.full((rows, 128), blocks, jnp.int32)
        for order in range(blocks):
            found = jnp.where(target[:, order : order + 1] == spots, order, found)
        return ((found ^ spots) & 1) * tiles + (found >> 1)

    agg = lax.broadcasted_iota(jnp.int32, (NB, KP), 0) >> 3
    slot = wrapped(cols_p - (device * NC + agg) + H, count_agg)
    agg_a = lax.broadcasted_iota(jnp.int32, (NB, KA), 0) >> 3
    fine = wrapped(cols_a - (device * NC + agg_a - 1) * AGG, count_agg * AGG)
    return (
        tile_of(slot + agg + 1 + odd, KP, 14),
        tile_of(slot[:AGG] + (5 - odd), KP, 14),
        tile_of(slot[NB - AGG :] + (1 - odd), KP, 14),
        tile_of(fine, KA, 4),
    )


def swap_halves(x):
    return jnp.concatenate([x[:, BS:], x[:, :BS]], axis=1)


def dot(a, b):
    return jnp.dot(a, b, preferred_element_type=F32)


def aligned(value, multiple=128):
    return pl.multiple_of(value, multiple)


def doubled(src, first, dst, wide, tiles, begin=0, end=AGG):
    def step(e, _):
        rows = pl.ds(aligned(e * BS, BS), BS)
        for tile in range(tiles):
            if 128 * (tile + 1) <= wide:
                here = src[first + e, :, 128 * tile : 128 * tile + 128]
            else:
                here = jnp.concatenate([src[first + e, :, 128 * tile : wide], jnp.zeros((BS, BS), BF16)], axis=1)
            dst[tile, rows, :] = here
            dst[tiles + tile, rows, :] = swap_halves(here)
        return 0

    lax.fori_loop(begin, end, step, 0)


def place(tab, first, src, dst, dst_row, pairs, begin=0, end=AGG):
    low = lax.broadcasted_iota(jnp.int32, (BS, 128), 1) < BS

    def step(e, _):
        rows = pl.ds(aligned(e * BS, BS), BS)
        to = pl.ds(aligned(dst_row + e * BS, BS), BS)
        for pair in range(pairs):
            left = src[tab[first + e, 2 * pair], rows, :]
            right = src[tab[first + e, 2 * pair + 1], rows, :]
            dst[to, 128 * pair : 128 * pair + 128] = jnp.where(low, left, right)
        return 0

    lax.fori_loop(begin, end, step, 0)


def chain_kernel(count, cols_a, cols_p, p_blocks, a_blocks, from_far, from_near, middle, *scratch):
    here_a, here_p, tab_made, tab, raw, raw_a, halo, halo_tab, tab_here, p2, a2, ext, pt, ad, w, wf, part = scratch[:17]
    to_far = [*scratch[17 : 17 + REACH], from_near]
    to_near = [*scratch[17 + REACH : 17 + 2 * REACH], from_far]
    load_sem, halo_send, halo_recv, send_far, recv_far, send_near, recv_near = scratch[17 + 2 * REACH :]
    me = lax.axis_index("dom")
    odd = lax.rem(me, 2)
    far, near = lax.rem(me + count - 1 + 2 * odd, count), lax.rem(me + count + 1 - 2 * odd, count)
    far_agg, near_agg = 2 * odd, 2 - 2 * odd

    def load(agg, slot, sem):
        return pltpu.make_async_copy(p_blocks.at[pl.ds(AGG * agg, AGG)], raw.at[slot], load_sem.at[sem])

    barrier = pltpu.get_barrier_semaphore()
    for neighbour in (far, near):
        pl.semaphore_signal(barrier, inc=1, device_id=(neighbour,), device_id_type=MESH)
    load_cols = [
        pltpu.make_async_copy(cols_a, here_a, load_sem.at[8]),
        pltpu.make_async_copy(cols_p, here_p, load_sem.at[9]),
    ]
    loads = [load(far_agg, 0, 0), load(near_agg, 1, 1)]
    load_a = pltpu.make_async_copy(a_blocks, raw_a, load_sem.at[2])
    for copy in (*load_cols, *loads, load_a):
        copy.start()

    def remote(src, dst, send_sem, recv_sem, target):
        return pltpu.make_async_remote_copy(
            src_ref=src, dst_ref=dst, send_sem=send_sem, recv_sem=recv_sem, device_id=(target,), device_id_type=MESH
        )

    def halo_copies(side, target, agg):
        copies = [
            remote(
                tab_made.at[pl.ds(aligned(NB + 4 * agg, 8), AGG)],
                halo_tab.at[side],
                halo_send.at[side, AGG // PIECE],
                halo_recv.at[side, AGG // PIECE],
                target,
            )
        ]
        for piece in range(AGG // PIECE):
            copies.append(
                remote(
                    p_blocks.at[pl.ds(AGG * agg + PIECE * piece, PIECE)],
                    halo.at[side, pl.ds(PIECE * piece, PIECE)],
                    halo_send.at[side, piece],
                    halo_recv.at[side, piece],
                    target,
                )
            )
        return copies

    halos = [halo_copies(0, far, far_agg), halo_copies(1, near, near_agg)]

    def own(agg):
        place(tab, AGG * agg, p2, ext, ROWS + ROWS * agg, 18)

    def arrived(side, edge):
        halos[side][0].wait_recv()
        pltpu.make_async_copy(halo_tab.at[side], tab_here.at[side], load_sem.at[5 + side]).start()
        pltpu.make_async_copy(halo_tab.at[side], tab_here.at[side], load_sem.at[5 + side]).wait()
        for piece in range(AGG // PIECE):
            rows = PIECE * piece, PIECE * (piece + 1)
            halos[side][1 + piece].wait_recv()
            doubled(halo.at[side], 0, p2, KP * BS, 14, *rows)
            place(tab_here.at[side], 0, p2, ext, 4 * ROWS * edge, 18, *rows)

    for copy in load_cols:
        copy.wait()
    at = 0
    for made in tables(here_a[...].T, here_p[...], me, NC * count):
        tab_made[at : at + made.shape[0], :] = made
        at += made.shape[0]
    load_tab = pltpu.make_async_copy(tab_made, tab, load_sem.at[7])
    load_tab.start()
    loads[0].wait()
    doubled(raw.at[0], 0, p2, KP * BS, 14)
    inner_load = load(1, 0, 3)
    inner_load.start()
    pl.semaphore_wait(barrier, 2)
    for copy in (*halos[0], *halos[1]):
        copy.start()
    load_tab.wait()
    own(far_agg)
    loads[1].wait()
    doubled(raw.at[1], 0, p2, KP * BS, 14)
    own(near_agg)
    inner_load.wait()
    doubled(raw.at[0], 0, p2, KP * BS, 14)
    own(1)
    load_a.wait()
    for agg in range(NC):
        doubled(raw_a, AGG * agg, a2, KA * BS, 4)
        place(tab, NB + 2 * AGG + AGG * agg, a2, ad, ROWS * agg, 12)

    for step in range(1, REACH):
        for buf, more, goes_right, before in (
            (to_far, 2 * BS, odd, NEAR_WIDTH[step - 1]),
            (to_near, 4 * BS, 1 - odd, FAR_WIDTH[step - 1]),
        ):
            buf[step][:, pl.ds(aligned(goes_right * before * BS), more)] = jnp.zeros((GROUP, more), BF16)

    def turn(tile):
        lanes = pl.ds(aligned(tile * 128), 128)
        for agg in range(NC):
            pt[lanes, ROWS * agg : ROWS * (agg + 1)] = ext[ROWS * (agg + 1) : ROWS * (agg + 2), lanes].T

    def chunks(body):
        def step(n, _):
            body(aligned(n * CHUNK))
            return 0

        lax.fori_loop(0, FRAME // CHUNK, step, 0)

    far_rows = pl.ds(aligned(far_agg * ROWS), ROWS)
    near_rows = pl.ds(aligned(near_agg * ROWS), ROWS)

    def inner(at):
        cols = pl.ds(at, CHUNK)
        w[ROWS : 2 * ROWS, cols] = dot(ad[ROWS : 2 * ROWS, :], ext[ROWS : 4 * ROWS, cols]).astype(BF16)
        wf[:, cols] = dot(
            ad[far_rows, pl.ds(aligned(ROWS * (1 - odd)), 2 * ROWS)],
            ext[pl.ds(aligned(ROWS + ROWS * odd), 2 * ROWS), cols],
        )

    def near_side(at):
        cols = pl.ds(at, CHUNK)
        whole = dot(ad[near_rows, :], ext[pl.ds(aligned(2 * ROWS * (1 - odd)), 3 * ROWS), cols])
        w[near_rows, cols] = whole.astype(BF16)

    def far_side(at):
        cols = pl.ds(at, CHUNK)
        more = dot(
            ad[far_rows, pl.ds(aligned(2 * ROWS * odd), ROWS)],
            ext[pl.ds(aligned(4 * ROWS * odd), ROWS), cols],
        )
        w[far_rows, cols] = (wf[:, cols] + more).astype(BF16)

    def product(group, at):
        rows = pl.ds(aligned((NC * group + 1 + odd) * BS, BS), GROUP)
        return dot(pt[rows, :], w[:, pl.ds(at, CHUNK)]).astype(BF16)

    def send(step, far_side, at=0, width=None, sem=None):
        buf, lands = (to_far, to_near) if far_side else (to_near, to_far)
        width = (FAR_WIDTH if far_side else NEAR_WIDTH)[step] * BS if width is None else width
        sem = step + FIRST - 1 if sem is None else sem
        grows = 0 if step == REACH - 1 else (4 * BS if far_side else 2 * BS)
        goes_left = 1 - odd if far_side else odd
        copy = remote(
            buf[step].at[:, pl.ds(at, width)],
            lands[step + 1].at[:, pl.ds(aligned(goes_left * grows + at), width)],
            (send_far if far_side else send_near).at[sem],
            (recv_far if far_side else recv_near).at[sem],
            far if far_side else near,
        )
        copy.start()
        return [copy]

    def far_product(step, at):
        return product(REACH + (REACH - step) * (2 * odd - 1), at)

    def near_product(step, at):
        return product(REACH - (REACH - step) * (2 * odd - 1), at)

    def add(buf, shift, side):
        def some(at):
            cols = pl.ds(aligned(at + shift * BS), CHUNK)
            summed = buf[:, cols].astype(F32) + part[side, :, pl.ds(at, CHUNK)].astype(F32)
            buf[:, cols] = summed.astype(BF16)

        chunks(some)

    def far_first(at):
        to_far[0][:, pl.ds(at, CHUNK)] = far_product(0, at)

    def near_first(at):
        to_near[0][:, pl.ds(at, CHUNK)] = near_product(0, at)

    for tile in range(2):
        turn(tile + 16 * odd)
        turn(tile + 15 - 14 * odd)
        turn(tile + 2 + 12 * odd)
    arrived(1, 1 - odd)

    def ready(at):
        inner(at)
        near_side(at)

    def some_chunks(n, _):
        ready(aligned(n * CHUNK))
        return 0

    lax.fori_loop(0, FIRST, some_chunks, 0)
    arrived(0, odd)
    far_sent, near_sent = [[]], [[]]
    for n in range(FIRST):
        at = n * CHUNK
        far_side(at)
        far_first(at)
        far_sent[0] += send(0, True, at, CHUNK, n)
        near_first(at)
        near_sent[0] += send(0, False, at, CHUNK, n)

    def turn_all(tile, _):
        turn(tile)
        return 0

    for step in range(REACH):
        if step == 1:
            lax.fori_loop(0, FRAME // 128, turn_all, 0)

        def prepare(at):
            cols = pl.ds(at, CHUNK)
            if step > 0:
                part[1, :, cols] = near_product(step, at)
            if step + 1 < REACH:
                part[0, :, cols] = far_product(step + 1, at)

        chunks(prepare)
        if step > 0:
            for copy in far_sent[step - 1]:
                copy.wait_recv()
            add(to_near[step], NEAR_SHIFT[step] * (1 - odd), 1)
            near_sent.append(send(step, False))
        if step + 1 < REACH:
            for copy in near_sent[step]:
                copy.wait_recv()
            add(to_far[step + 1], FAR_SHIFT[step + 1] * odd, 0)
            far_sent.append(send(step + 1, True))

    def centre(at):
        part[0, :, pl.ds(at, CHUNK)] = product(REACH, at)

    chunks(centre)
    keep = pltpu.make_async_copy(part.at[0], middle, load_sem.at[4])
    keep.start()
    for copies in (*halos, *far_sent, *near_sent):
        for copy in copies:
            copy.wait_send()
    keep.wait()
    near_sent[-1][0].wait_recv()
    far_sent[-1][0].wait_recv()


def chain(count, cols_a, cols_p, p_blocks, a_blocks):
    anywhere = pl.BlockSpec(memory_space=pl.ANY)
    sums = [pltpu.VMEM((GROUP, width * BS), BF16) for width in (*FAR_WIDTH, *NEAR_WIDTH)]
    return pl.pallas_call(
        functools.partial(chain_kernel, count),
        out_shape=(
            jax.ShapeDtypeStruct((GROUP, WIDE), BF16),
            jax.ShapeDtypeStruct((GROUP, WIDE), BF16),
            jax.ShapeDtypeStruct((GROUP, FRAME), BF16),
        ),
        in_specs=[anywhere] * 4,
        out_specs=[anywhere] * 3,
        scratch_shapes=[
            pltpu.VMEM((KA, NB), jnp.int32),
            pltpu.VMEM((NB, KP), jnp.int32),
            pltpu.VMEM((2 * NB + 2 * AGG, 128), jnp.int32),
            pltpu.SMEM((2 * NB + 2 * AGG, 128), jnp.int32),
            pltpu.VMEM((2, AGG, BS, KP * BS), BF16),
            pltpu.VMEM((NB, BS, KA * BS), BF16),
            pltpu.VMEM((2, AGG, BS, KP * BS), BF16),
            pltpu.VMEM((2, AGG, 128), jnp.int32),
            pltpu.SMEM((2, AGG, 128), jnp.int32),
            pltpu.VMEM((2 * 14, ROWS, 128), BF16),
            pltpu.VMEM((2 * 4, ROWS, 128), BF16),
            pltpu.VMEM((5 * ROWS, FRAME), BF16),
            pltpu.VMEM((FRAME, 3 * ROWS), BF16),
            pltpu.VMEM((3 * ROWS, 3 * ROWS), BF16),
            pltpu.VMEM((3 * ROWS, FRAME), BF16),
            pltpu.VMEM((ROWS, FRAME), F32),
            pltpu.VMEM((2, GROUP, FRAME), BF16),
            *sums,
            pltpu.SemaphoreType.DMA((10,)),
            pltpu.SemaphoreType.DMA((2, AGG // PIECE + 1)),
            pltpu.SemaphoreType.DMA((2, AGG // PIECE + 1)),
            pltpu.SemaphoreType.DMA((REACH + FIRST - 1,)),
            pltpu.SemaphoreType.DMA((REACH + FIRST - 1,)),
            pltpu.SemaphoreType.DMA((REACH + FIRST - 1,)),
            pltpu.SemaphoreType.DMA((REACH + FIRST - 1,)),
        ],
        compiler_params=pltpu.CompilerParams(
            collective_id=0, has_side_effects=True, vmem_limit_bytes=63 * 2**20
        ),
    )(cols_a, cols_p, p_blocks, a_blocks)


def gather_kernel(from_far, from_near, middle, out, far_ref, near_ref, middle_ref, out_ref, load_sem, store_sem):
    odd = lax.rem(lax.axis_index("dom"), 2)
    pairs = ((from_far, far_ref), (from_near, near_ref), (middle, middle_ref))
    loads = [
        [
            pltpu.make_async_copy(src.at[pl.ds(BS * row, BS)], dst.at[row], load_sem.at[row, kind])
            for kind, (src, dst) in enumerate(pairs)
        ]
        for row in range(NC)
    ]
    stores = [pltpu.make_async_copy(out_ref.at[row], out.at[row], store_sem.at[row]) for row in range(NC)]
    for copies in loads:
        for copy in copies:
            copy.start()

    def write(row, parity):
        first = row + 1 - parity
        parts = [
            (near_ref if parity else far_ref, 0, 48),
            (middle_ref, 16 - 2 * parity, 52 - 2 * parity),
            (far_ref if parity else near_ref, 18, 66),
        ]
        edges = sorted({edge for _, begin, end in parts for edge in (begin, end)})
        for begin, end in zip(edges[:-1], edges[1:]):
            terms = [
                ref[row, :, (begin - left) * BS : (end - left) * BS].astype(F32)
                for ref, left, right in parts
                if left <= begin and end <= right
            ]
            value = functools.reduce(jnp.add, terms)
            low, high = max(begin, first), min(end, first + BAND)
            out_ref[row, :, (low - first) * BS : (high - first) * BS] = value[:, (low - begin) * BS : (high - begin) * BS]

    for row in range(NC):
        for copy in loads[row]:
            copy.wait()
        for parity in (0, 1):
            pl.when(odd == parity)(functools.partial(write, row, parity))
        stores[row].start()
    for copy in stores:
        copy.wait()


def gather(from_far, from_near, middle):
    anywhere = pl.BlockSpec(memory_space=pl.ANY)
    return pl.pallas_call(
        gather_kernel,
        out_shape=jax.ShapeDtypeStruct((NC, BS, BAND * BS), F32),
        in_specs=[anywhere] * 3,
        out_specs=anywhere,
        scratch_shapes=[
            pltpu.VMEM((NC, BS, WIDE), BF16),
            pltpu.VMEM((NC, BS, WIDE), BF16),
            pltpu.VMEM((NC, BS, FRAME), BF16),
            pltpu.VMEM((NC, BS, BAND * BS), F32),
            pltpu.SemaphoreType.DMA((NC, 3)),
            pltpu.SemaphoreType.DMA((NC,)),
        ],
        compiler_params=pltpu.CompilerParams(vmem_limit_bytes=62 * 2**20),
    )(from_far, from_near, middle)


def body(a_blocks, p_blocks, cols_a, cols_p):
    count = lax.axis_size("dom")
    return gather(*chain(count, cols_a.T, cols_p, p_blocks, a_blocks))


def solution(mesh):
    in_specs = (P("dom", None, None), P("dom", None, None), P("dom", None), P("dom", None))
    out_specs = P("dom", None, None)
    return jax.shard_map(body, mesh=mesh, in_specs=in_specs, out_specs=out_specs, check_vma=False)
```
